256 devices in a mesh: gx: 128 (over x, z, y), bl: 2 (over core).
Axes of the slice: x: 4, y: 4, z: 8, core: 2. Of those that a mesh axis runs over, the one named last changes fastest.
Arguments:
- voltages: bfloat16 [2, 1024, 71680], P('bl', 'gx'), may hold values from -10 to 10, as said below
- model_magnitude: float32 [128, 2048], P('gx'), may hold values from 0.06 to 0.25
- model_phase: float32 [128, 2048], P('gx'), may hold values from -3.140625 to 3.140625
Outputs:
- visibilities: bfloat16 [128, 2, 2048, 2048], P('gx', None, 'bl')
- gains: float32 [2, 2, 1024, 128], P(None, 'bl', 'gx')
The draws below stay inside these ranges and needn't reach their ends.
Inputs may be any that keep to these rules, and one draw needn't show every extreme that they name: `voltages`: each input's sampled voltage stream.
All inputs are finite; a program needn't handle non-finite values.
Results may differ from the reference program's by a relative error of at most 0.0057.
Values may be sent and summed in bfloat16 or wider, within the bound.
No kernel may reach another device: no remote copies, remote signals or barrier semaphores. Data moves between devices by JAX's collectives and lax.ppermute only.
A program may use at most 64 MiB of HBM per device.

```python
import math
import jax
import jax.numpy as jnp
from jax import lax

INPUTS = 2048
NFFT = 2048
TAPS = 4
SPECTRA = 32
ITERS = 4
CHANNELS = 128
TILES = 2
HALF = 1024
SAMPLES = 71680
STRIDE = 8


def draw_voltages(key, part):
    key_strength = jax.random.fold_in(jax.random.fold_in(key, 17), 0)
    key_source = jax.random.fold_in(jax.random.fold_in(key, 17), 1)
    key_noise = jax.random.fold_in(jax.random.fold_in(key, 17), 3)
    strength = jnp.exp(jax.random.uniform(key_strength, (TILES, HALF, 1), jnp.float32, math.log(0.12), math.log(0.4)))
    source = jax.random.truncated_normal(key_source, -4.0, 4.0, (1, 1, SAMPLES), jnp.float32)
    noise_part = 2.0 * jax.random.truncated_normal(key_noise, -4.0, 4.0, (TILES, HALF, SAMPLES), jnp.float32)
    return (noise_part + strength * source).astype(jnp.bfloat16)


def level_of(own_key, shape, shards, low, high):
    factor_of = 1.0
    for axis_at, parts in shards:
        draws = jax.random.uniform(jax.random.fold_in(jax.random.fold_in(own_key, 6), axis_at), (parts,), jnp.float32, low / len(shards), high / len(shards))
        factor_of = factor_of * jnp.repeat(jnp.exp(draws), shape[axis_at] // parts).reshape((-1,) + (1,) * (len(shape) - 1 - axis_at))
    return factor_of


def setup_inputs(seed: int = 0) -> dict:
    key_list = jax.random.split(jax.random.key(seed), 4)
    return {
        "voltages": draw_voltages(jax.random.fold_in(key_list[3], 71), 0),
        "model_magnitude": jnp.clip(jnp.exp(math.log(0.25) - 1.4271164 * jax.random.uniform(key_list[1], (CHANNELS, INPUTS), jnp.float32) ** level_of(key_list[1], (CHANNELS, INPUTS), ((0, 128),), -0.2, 0.2)), 0.06, 0.25),
        "model_phase": jnp.clip(jax.random.uniform(key_list[2], (CHANNELS, INPUTS), jnp.float32, -3.140625, 3.140625), -3.140625, 3.140625),
    }


def window_table(tap_count, length):
    positions = jnp.arange(tap_count * length, dtype=jnp.float32)
    centre = (positions + 0.5) / length - tap_count / 2.0
    hann_taper = 0.5 - 0.5 * jnp.cos(2.0 * math.pi * (positions + 0.5) / (tap_count * length))
    return (jnp.sinc(centre) * hann_taper).reshape(tap_count, length)

def reference(voltages, model_magnitude, model_phase):
    frames_total = SPECTRA + TAPS - 1
    taps_window = window_table(TAPS, NFFT)
    bin_index = (jnp.arange(CHANNELS, dtype=jnp.int32) * STRIDE + (STRIDE + 1) // 2).astype(jnp.int32)

    def channelize(row_block):
        framed = row_block.reshape(row_block.shape[0], frames_total, NFFT).astype(jnp.float32)
        summed = framed[:, 0:SPECTRA, :] * taps_window[0]
        for tap_index in range(1, TAPS):
            summed = summed + framed[:, tap_index:tap_index + SPECTRA, :] * taps_window[tap_index]
        spectrum = jnp.fft.rfft(summed, axis=2)
        picked = jnp.take(spectrum, bin_index, axis=2)
        real_part = (jnp.real(picked) / math.sqrt(NFFT)).astype(jnp.float32)
        imag_part = (jnp.imag(picked) / math.sqrt(NFFT)).astype(jnp.float32)
        return jnp.stack([real_part, imag_part], axis=0).astype(jnp.bfloat16)
    row_blocks = voltages.reshape(INPUTS // 64, 64, SAMPLES)
    channelized = lax.map(channelize, row_blocks)
    spectra_all = jnp.transpose(channelized, (4, 1, 0, 2, 3)).reshape(CHANNELS, 2, INPUTS, SPECTRA)
    identity = jnp.arange(INPUTS)[:, None] == jnp.arange(INPUTS)[None, :]

    def per_channel(packed):
        spectra_one, magnitude, phase_row = packed
        dense_values = spectra_one.astype(jnp.float32)
        left_side = jnp.concatenate([dense_values[0], dense_values[1]], axis=1)
        lower_side = jnp.concatenate([dense_values[1], -dense_values[0]], axis=1)
        real_power = jnp.dot(left_side, left_side.T, precision=lax.Precision.HIGHEST) * (1.0 / SPECTRA)
        imag_power = jnp.dot(lower_side, left_side.T, precision=lax.Precision.HIGHEST) * (1.0 / SPECTRA)
        hollow_real = jnp.where(identity, jnp.float32(0.0), real_power)
        hollow_imag = jnp.where(identity, jnp.float32(0.0), imag_power)
        model_real = magnitude * jnp.cos(phase_row)
        model_imag = magnitude * jnp.sin(phase_row)
        inverse_square = 1.0 / (magnitude * magnitude)
        gain_real = jnp.ones((INPUTS,), jnp.float32)
        gain_imag = jnp.zeros((INPUTS,), jnp.float32)
        for step_index in range(ITERS):
            probe_real = gain_real * model_real - gain_imag * model_imag
            probe_imag = gain_real * model_imag + gain_imag * model_real
            image_real = jnp.dot(hollow_real, probe_real, precision=lax.Precision.HIGHEST) - jnp.dot(hollow_imag, probe_imag, precision=lax.Precision.HIGHEST)
            image_imag = jnp.dot(hollow_real, probe_imag, precision=lax.Precision.HIGHEST) + jnp.dot(hollow_imag, probe_real, precision=lax.Precision.HIGHEST)
            energy = jnp.sum(probe_real * probe_real + probe_imag * probe_imag) + 1e-06
            factor = inverse_square / energy
            fresh_real = (image_real * model_real + image_imag * model_imag) * factor
            fresh_imag = (image_imag * model_real - image_real * model_imag) * factor
            if step_index % 2 == 1:
                gain_real = (fresh_real + gain_real) * 0.5
                gain_imag = (fresh_imag + gain_imag) * 0.5
            else:
                gain_real = fresh_real
                gain_imag = fresh_imag
        visible = jnp.stack([real_power, imag_power], axis=0).astype(jnp.bfloat16)
        return (visible, jnp.stack([gain_real, gain_imag], axis=0))
    visibilities, gain_table = lax.map(per_channel, (spectra_all, model_magnitude, model_phase))
    gains = jnp.transpose(gain_table, (1, 2, 0)).reshape(2, TILES, HALF, CHANNELS)
    return (visibilities, gains)
```

```python
import functools
import math

import jax
import jax.numpy as jnp
import numpy as np
from jax import lax
from jax.experimental import pallas as pl
from jax.experimental.pallas import tpu as pltpu
from jax.sharding import PartitionSpec as P

NFFT = 2048
TAPS = 4
SPECTRA = 32
ITERS = 4
CHANNELS = 128
OWNED = 8
EPSILON = 1e-06
F32 = jnp.float32
BF16 = jnp.bfloat16
FOLD = 256
FOLDS = NFFT // FOLD


def split_bf16(values):
    high = values.astype(np.float32).astype(jnp.bfloat16)
    low = (values - high.astype(np.float64)).astype(np.float32).astype(jnp.bfloat16)
    return high, low


def fold_weights():
    position = np.arange(TAPS * NFFT, dtype=np.float64) + 0.5
    hann = 0.5 - 0.5 * np.cos(2.0 * np.pi * position / (TAPS * NFFT))
    taper = np.sinc(position / NFFT - TAPS / 2.0) * hann
    taper = taper.reshape(TAPS, FOLDS, FOLD)
    signs = (-1.0) ** np.arange(FOLDS)
    folded = (taper * signs[None, :, None]).transpose(1, 0, 2)
    return folded.astype(np.float32)


def transform_weights():
    odd = 2 * np.arange(CHANNELS) + 1
    phase = (odd[:, None] * np.arange(FOLD)[None, :]) % (2 * FOLD)
    angle = phase.astype(np.float64) * (2.0 * np.pi / (2 * FOLD))
    scale = 1.0 / math.sqrt(NFFT)
    table = np.concatenate([np.cos(angle), -np.sin(angle)], axis=0) * scale
    high, low = split_bf16(table)
    return np.concatenate([high, high, low], axis=1)


def channelize_kernel(volts_ref, window_ref, table_ref, out_ref, folded_ref, rows_ref):
    for part in range(FOLD // 128):

        def fold_step(fold, sums):
            start = pl.multiple_of(fold * FOLD + part * 128, 128)
            taps = [
                jnp.broadcast_to(
                    window_ref[fold, tap : tap + 1, part * 128 : part * 128 + 128],
                    (OWNED, 128),
                )
                for tap in range(TAPS)
            ]
            sums = list(sums)
            for frame in range(SPECTRA + TAPS - 1):
                piece = volts_ref[:, pl.ds(start + frame * NFFT, 128)].astype(F32)
                for tap in range(TAPS):
                    s = frame - tap
                    if 0 <= s < SPECTRA:
                        sums[s] = sums[s] + piece * taps[tap]
            return tuple(sums)

        zero = jnp.zeros((OWNED, 128), F32)
        sums = lax.fori_loop(0, FOLDS, fold_step, (zero,) * SPECTRA)
        for s in range(SPECTRA):
            folded_ref[part, pl.ds(s * OWNED, OWNED), :] = sums[s]
    pieces = []
    for part in range(FOLD // 128):
        pieces.append(
            jnp.concatenate(
                [folded_ref[part, pl.ds(j, SPECTRA, OWNED), :] for j in range(OWNED)],
                axis=0,
            )
        )
    folded = jnp.concatenate(pieces, axis=1)
    high = folded.astype(BF16)
    low = (folded - high.astype(F32)).astype(BF16)
    right = jnp.concatenate([high, low, high], axis=1)
    spectra = lax.dot_general(
        table_ref[...], right, (((1,), (1,)), ((), ())), preferred_element_type=F32
    )
    for part in range(2):
        for side in range(2):
            rows_ref[pl.ds(part * 2 + side, CHANNELS, 4), :] = spectra[
                part * CHANNELS : (part + 1) * CHANNELS, side * 128 : side * 128 + 128
            ]
    out_ref[...] = rows_ref[...].astype(BF16)


def channelize(volts):
    return pl.pallas_call(
        channelize_kernel,
        out_shape=jax.ShapeDtypeStruct((CHANNELS * 4, 128), BF16),
        scratch_shapes=[
            pltpu.VMEM((2, SPECTRA * OWNED, 128), F32),
            pltpu.VMEM((CHANNELS * 4, 128), F32),
        ],
        compiler_params=pltpu.CompilerParams(vmem_limit_bytes=16 * 2**20),
        name="channelize",
    )(volts, jnp.asarray(fold_weights()), jnp.asarray(transform_weights()))


def solve_kernel(
    own_ref, other_ref, mreal_ref, mimag_ref, inverse_ref, out_ref,
    wide_ref, xr_ref, xi_ref, probe_ref, part_ref,
):
    half = lax.axis_index("bl")
    for side, source in ((0, own_ref), (1, other_ref)):
        tile = half if side == 0 else 1 - half
        wide_ref[...] = source[...].astype(F32)
        for part in range(2):
            target = xr_ref if part == 0 else xi_ref
            for group in range(2):
                block = wide_ref[pl.ds(part * 2 + group, 128, 4), :].T
                for j in range(4):
                    target[tile * OWNED + group * 4 + j] = block[j * 32 : j * 32 + 32, :]
    tiles = 2 * OWNED

    def gathered(which):
        total = part_ref[which, pl.ds(0, tiles, 8), :]
        for row in range(1, 8):
            total = total + part_ref[which, pl.ds(row, tiles, 8), :]
        return total

    def eight(values):
        return (values[0:8] + values[8:16]) + (values[16:24] + values[24:32])

    for tile in range(tiles):
        real, imag = xr_ref[tile], xi_ref[tile]
        part_ref[0, tile * 8 : tile * 8 + 8, :] = eight(real * real + imag * imag)
    diagonal = gathered(0) * (1.0 / SPECTRA)
    mreal, mimag, inverse = mreal_ref[...], mimag_ref[...], inverse_ref[...]

    def single_step(greal, gimag):
        yreal = greal * mreal - gimag * mimag
        yimag = greal * mimag + gimag * mreal
        energy = jnp.sum(yreal * yreal + yimag * yimag, keepdims=True) + EPSILON
        factor = inverse / energy
        probe_ref[0] = yreal
        probe_ref[1] = yimag
        areal = jnp.zeros((SPECTRA, 128), F32)
        aimag = jnp.zeros((SPECTRA, 128), F32)
        for tile in range(tiles):
            real, imag = xr_ref[tile], xi_ref[tile]
            pr = jnp.broadcast_to(probe_ref[0, tile : tile + 1, :], (SPECTRA, 128))
            pi = jnp.broadcast_to(probe_ref[1, tile : tile + 1, :], (SPECTRA, 128))
            areal = areal + (real * pr + imag * pi)
            aimag = aimag + (real * pi - imag * pr)
        sreal = jnp.broadcast_to(jnp.sum(areal, axis=1, keepdims=True), (SPECTRA, 128))
        simag = jnp.broadcast_to(jnp.sum(aimag, axis=1, keepdims=True), (SPECTRA, 128))
        for tile in range(tiles):
            real, imag = xr_ref[tile], xi_ref[tile]
            rows = slice(tile * 8, tile * 8 + 8)
            part_ref[0, rows, :] = eight(real * sreal - imag * simag)
            part_ref[1, rows, :] = eight(real * simag + imag * sreal)
        wreal = gathered(0) * (1.0 / SPECTRA) - diagonal * yreal
        wimag = gathered(1) * (1.0 / SPECTRA) - diagonal * yimag
        return (
            (wreal * mreal + wimag * mimag) * factor,
            (wimag * mreal - wreal * mimag) * factor,
        )

    greal = jnp.ones((tiles, 128), F32)
    gimag = jnp.zeros((tiles, 128), F32)

    def double_step(_, gains):
        first = single_step(*gains)
        fresh = single_step(*first)
        return tuple((a + b) * 0.5 for a, b in zip(fresh, first))

    greal, gimag = lax.fori_loop(0, ITERS // 2, double_step, (greal, gimag))
    probe_ref[0] = greal
    probe_ref[1] = gimag
    start = pl.multiple_of(half * OWNED, OWNED)
    wide_ref[0:128, :] = jnp.zeros((128, 128), F32)
    wide_ref[0:8, :] = probe_ref[0, pl.ds(start, OWNED), :]
    wide_ref[8:16, :] = probe_ref[1, pl.ds(start, OWNED), :]
    out_ref[...] = wide_ref[0:128, :].T


def solve(own, other, mreal, mimag, inverse):
    tiles = 2 * OWNED
    return pl.pallas_call(
        solve_kernel,
        out_shape=jax.ShapeDtypeStruct((128, 128), F32),
        scratch_shapes=[
            pltpu.VMEM((512, 128), F32),
            pltpu.VMEM((tiles, SPECTRA, 128), F32),
            pltpu.VMEM((tiles, SPECTRA, 128), F32),
            pltpu.VMEM((2, tiles, 128), F32),
            pltpu.VMEM((2, tiles * 8, 128), F32),
        ],
        compiler_params=pltpu.CompilerParams(vmem_limit_bytes=16 * 2**20),
        name="solve",
    )(own, other, mreal, mimag, inverse)


ROWS = 128


def power_kernel(own_ref, other_ref, out_ref, wide_ref, line_ref, upper_ref, lower_ref, right_ref):
    half = lax.axis_index("bl")
    step = pl.program_id(0)

    @pl.when(step == 0)
    def _():
        for side, source in ((0, own_ref), (1, other_ref)):
            tile = half if side == 0 else 1 - half
            wide_ref[...] = source[...].astype(F32)
            for group in range(2):
                real = wide_ref[pl.ds(group, 128, 4), :]
                imag = wide_ref[pl.ds(2 + group, 128, 4), :]
                for j in range(4):
                    a = real[:, j * 32 : j * 32 + 32]
                    b = imag[:, j * 32 : j * 32 + 32]
                    line_ref[pl.ds(group * 4 + j, 128, OWNED), :] = jnp.concatenate(
                        [a, b, b, -a], axis=1
                    )
            lines = line_ref[...]
            start = pl.multiple_of(tile * 1024, 1024)
            right_ref[pl.ds(start, 1024), :] = lines[:, 0:64].astype(BF16)
            if side == 0:
                scaled = lines * (1.0 / SPECTRA)
                upper_ref[...] = scaled[:, 0:64].astype(BF16)
                lower_ref[...] = scaled[:, 64:128].astype(BF16)

    rows = pl.ds(pl.multiple_of(step * ROWS, ROWS), ROWS)
    for part, left in ((0, upper_ref), (1, lower_ref)):
        out_ref[part] = lax.dot_general(
            left[rows, :], right_ref[...], (((1,), (1,)), ((), ())),
            preferred_element_type=F32,
        ).astype(BF16)


def power(own, other):
    return pl.pallas_call(
        power_kernel,
        grid=(1024 // ROWS,),
        in_specs=[pl.BlockSpec((512, 128), lambda s: (0, 0))] * 2,
        out_specs=pl.BlockSpec((2, ROWS, 2048), lambda s: (0, s, 0)),
        out_shape=jax.ShapeDtypeStruct((2, 1024, 2048), BF16),
        scratch_shapes=[
            pltpu.VMEM((512, 128), F32),
            pltpu.VMEM((1024, 128), F32),
            pltpu.VMEM((1024, 64), BF16),
            pltpu.VMEM((1024, 64), BF16),
            pltpu.VMEM((2048, 64), BF16),
        ],
        compiler_params=pltpu.CompilerParams(vmem_limit_bytes=24 * 2**20),
        cost_estimate=pl.CostEstimate(
            flops=2 * 2 * 1024 * 2048 * 64, bytes_accessed=9 * 2**20, transcendentals=0
        ),
        name="power",
    )(own, other)


def turn_kernel(gains_ref, out_ref):
    turned = gains_ref[...].T
    out_ref[0, 0] = turned[0:8, :]
    out_ref[1, 0] = turned[8:16, :]


def on_device(voltages, model_magnitude, model_phase):
    spectra = channelize(voltages[0])
    own = lax.all_to_all(spectra.reshape(CHANNELS, 4, 128), "gx", 0, 0)
    own = own.reshape(512, 128)
    other = lax.ppermute(own, "bl", [(0, 1), (1, 0)])

    def tiles(values):
        return values.reshape(2, 128, OWNED).transpose(0, 2, 1).reshape(2 * OWNED, 128)

    mreal = tiles(model_magnitude * jnp.cos(model_phase))
    mimag = tiles(model_magnitude * jnp.sin(model_phase))
    inverse = tiles(1.0 / (model_magnitude * model_magnitude))
    gains = solve(own, other, mreal, mimag, inverse)
    moved = lax.all_to_all(gains.reshape(128, 1, 128), "gx", 0, 0)
    visible = power(own, other)
    gain_output = pl.pallas_call(
        turn_kernel,
        out_shape=jax.ShapeDtypeStruct((2, 1, OWNED, CHANNELS), F32),
        name="turn",
    )(moved.reshape(128, 128))
    return visible[None], gain_output


def solution(mesh):
    in_specs = (P("bl", "gx", None), P("gx", None), P("gx", None))
    out_specs = (P("gx", None, "bl", None), P(None, "bl", "gx", None))
    return jax.shard_map(
        on_device, mesh=mesh, in_specs=in_specs, out_specs=out_specs, check_vma=False
    )
```

```python
import functools
import math

import jax
import jax.numpy as jnp
import numpy as np
from jax import lax
from jax.experimental import pallas as pl
from jax.experimental.pallas import tpu as pltpu
from jax.sharding import PartitionSpec as P

NFFT = 2048
TAPS = 4
SPECTRA = 32
ITERS = 4
CHANNELS = 128
OWNED = 8
EPSILON = 1e-06
F32 = jnp.float32
BF16 = jnp.bfloat16
FOLD = 256
FOLDS = NFFT // FOLD


def split_bf16(values):
    high = values.astype(np.float32).astype(jnp.bfloat16)
    low = (values - high.astype(np.float64)).astype(np.float32).astype(jnp.bfloat16)
    return high, low


def fold_weights():
    position = np.arange(TAPS * NFFT, dtype=np.float64) + 0.5
    hann = 0.5 - 0.5 * np.cos(2.0 * np.pi * position / (TAPS * NFFT))
    taper = np.sinc(position / NFFT - TAPS / 2.0) * hann
    taper = taper.reshape(TAPS, FOLDS, FOLD)
    signs = (-1.0) ** np.arange(FOLDS)
    folded = (taper * signs[None, :, None]).transpose(1, 0, 2)
    return folded.astype(np.float32)


def transform_weights():
    odd = 2 * np.arange(CHANNELS) + 1
    phase = (odd[:, None] * np.arange(FOLD)[None, :]) % (2 * FOLD)
    angle = phase.astype(np.float64) * (2.0 * np.pi / (2 * FOLD))
    scale = 1.0 / math.sqrt(NFFT)
    table = np.concatenate([np.cos(angle), -np.sin(angle)], axis=0) * scale
    high, low = split_bf16(table)
    return np.concatenate([high, low], axis=1)


GROUP = 8
GROUPS = SPECTRA // GROUP


def channelize_kernel(
    volts_hbm, window_hbm, table_hbm, out_ref,
    volts_ref, window_ref, table_ref, folded_ref, rows_ref, sems,
):
    def frames_copy(group):
        first = 0 if group == 0 else group * GROUP + TAPS - 1
        last = (group + 1) * GROUP + TAPS - 1
        span = pl.ds(first * NFFT, (last - first) * NFFT)
        return pltpu.make_async_copy(
            volts_hbm.at[:, span], volts_ref.at[:, span], sems.at[group]
        )

    window_copy = pltpu.make_async_copy(window_hbm, window_ref, sems.at[GROUPS])
    table_copy = pltpu.make_async_copy(table_hbm, table_ref, sems.at[GROUPS + 1])
    window_copy.start()
    for group in range(GROUPS):
        frames_copy(group).start()
    table_copy.start()
    window_copy.wait()
    for group in range(GROUPS):
        frames_copy(group).wait()
        for part in range(FOLD // 128):

            def fold_step(fold, sums):
                start = pl.multiple_of(fold * FOLD + part * 128, 128)
                taps = [
                    jnp.broadcast_to(
                        window_ref[fold, tap : tap + 1, part * 128 : part * 128 + 128],
                        (OWNED, 128),
                    )
                    for tap in range(TAPS)
                ]
                sums = list(sums)
                for frame in range(GROUP + TAPS - 1):
                    offset = start + (group * GROUP + frame) * NFFT
                    piece = volts_ref[:, pl.ds(offset, 128)].astype(F32)
                    for tap in range(TAPS):
                        s = frame - tap
                        if 0 <= s < GROUP:
                            sums[s] = sums[s] + piece * taps[tap]
                return tuple(sums)

            zero = jnp.zeros((OWNED, 128), F32)
            sums = lax.fori_loop(0, FOLDS, fold_step, (zero,) * GROUP, unroll=2)
            for s in range(GROUP):
                folded_ref[part, pl.ds((group * GROUP + s) * OWNED, OWNED), :] = sums[s]
    pieces = []
    for part in range(FOLD // 128):
        pieces.append(
            jnp.concatenate(
                [folded_ref[part, pl.ds(j, SPECTRA, OWNED), :] for j in range(OWNED)],
                axis=0,
            )
        )
    folded = jnp.concatenate(pieces, axis=1)
    high = folded.astype(BF16)
    low = (folded - high.astype(F32)).astype(BF16)
    table_copy.wait()
    across = (((1,), (1,)), ((), ()))
    spectra = (
        lax.dot_general(table_ref[:, 0:FOLD], high, across, preferred_element_type=F32)
        + lax.dot_general(table_ref[:, 0:FOLD], low, across, preferred_element_type=F32)
        + lax.dot_general(
            table_ref[:, FOLD : 2 * FOLD], high, across, preferred_element_type=F32
        )
    )
    for part in range(2):
        for side in range(2):
            rows_ref[pl.ds(part * 2 + side, CHANNELS, 4), :] = spectra[
                part * CHANNELS : (part + 1) * CHANNELS, side * 128 : side * 128 + 128
            ]
    out_ref[...] = rows_ref[...].astype(BF16)


def channelize(volts):
    return pl.pallas_call(
        channelize_kernel,
        out_shape=jax.ShapeDtypeStruct((CHANNELS * 4, 128), BF16),
        in_specs=[pl.BlockSpec(memory_space=pltpu.HBM)] * 3,
        scratch_shapes=[
            pltpu.VMEM(volts.shape, BF16),
            pltpu.VMEM((FOLDS, TAPS, FOLD), F32),
            pltpu.VMEM((2 * CHANNELS, 2 * FOLD), BF16),
            pltpu.VMEM((2, SPECTRA * OWNED, 128), F32),
            pltpu.VMEM((CHANNELS * 4, 128), F32),
            pltpu.SemaphoreType.DMA((GROUPS + 2,)),
        ],
        compiler_params=pltpu.CompilerParams(vmem_limit_bytes=58 * 2**20),
        name="channelize",
    )(volts, jnp.asarray(fold_weights()), jnp.asarray(transform_weights()))


def turn_spectra(source, wide_ref, real_ref, imag_ref):
    wide_ref[...] = source[...].astype(F32)
    for part, target in ((0, real_ref), (1, imag_ref)):
        for group in range(2):
            block = wide_ref[pl.ds(part * 2 + group, 128, 4), :].T
            for j in range(4):
                target[group * 4 + j] = block[j * 32 : j * 32 + 32, :]


def own_kernel(own_ref, real_ref, imag_ref, wide_ref):
    turn_spectra(own_ref, wide_ref, real_ref, imag_ref)


def own_turn(own):
    return pl.pallas_call(
        own_kernel,
        out_shape=[jax.ShapeDtypeStruct((OWNED, SPECTRA, 128), F32)] * 2,
        scratch_shapes=[pltpu.VMEM((512, 128), F32)],
        compiler_params=pltpu.CompilerParams(vmem_limit_bytes=4 * 2**20),
        cost_estimate=pl.CostEstimate(
            flops=2**22, bytes_accessed=2**20, transcendentals=0
        ),
        name="own_turn",
    )(own)


def solve_kernel(
    ownr_ref, owni_ref, other_ref, mreal_ref, mimag_ref, inverse_ref, out_ref,
    wide_ref, otherr_ref, otheri_ref, probe_ref, part_ref,
):
    turn_spectra(other_ref, wide_ref, otherr_ref, otheri_ref)
    tiles = 2 * OWNED

    def spectra_of(tile):
        if tile < OWNED:
            return ownr_ref[tile], owni_ref[tile]
        return otherr_ref[tile - OWNED], otheri_ref[tile - OWNED]

    def gathered(which):
        total = part_ref[which, pl.ds(0, tiles, 8), :]
        for row in range(1, 8):
            total = total + part_ref[which, pl.ds(row, tiles, 8), :]
        return total

    def eight(values):
        return (values[0:8] + values[8:16]) + (values[16:24] + values[24:32])

    for tile in range(tiles):
        real, imag = spectra_of(tile)
        part_ref[0, tile * 8 : tile * 8 + 8, :] = eight(real * real + imag * imag)
    diagonal = gathered(0) * (1.0 / SPECTRA)
    mreal, mimag, inverse = mreal_ref[...], mimag_ref[...], inverse_ref[...]

    def single_step(greal, gimag):
        yreal = greal * mreal - gimag * mimag
        yimag = greal * mimag + gimag * mreal
        energy = jnp.sum(yreal * yreal + yimag * yimag, keepdims=True) + EPSILON
        factor = inverse / energy
        probe_ref[0] = yreal
        probe_ref[1] = yimag
        areal = jnp.zeros((SPECTRA, 128), F32)
        aimag = jnp.zeros((SPECTRA, 128), F32)
        for tile in range(tiles):
            real, imag = spectra_of(tile)
            pr = jnp.broadcast_to(probe_ref[0, tile : tile + 1, :], (SPECTRA, 128))
            pi = jnp.broadcast_to(probe_ref[1, tile : tile + 1, :], (SPECTRA, 128))
            areal = areal + (real * pr + imag * pi)
            aimag = aimag + (real * pi - imag * pr)
        sreal = jnp.broadcast_to(jnp.sum(areal, axis=1, keepdims=True), (SPECTRA, 128))
        simag = jnp.broadcast_to(jnp.sum(aimag, axis=1, keepdims=True), (SPECTRA, 128))
        for tile in range(tiles):
            real, imag = spectra_of(tile)
            rows = slice(tile * 8, tile * 8 + 8)
            part_ref[0, rows, :] = eight(real * sreal - imag * simag)
            part_ref[1, rows, :] = eight(real * simag + imag * sreal)
        wreal = gathered(0) * (1.0 / SPECTRA) - diagonal * yreal
        wimag = gathered(1) * (1.0 / SPECTRA) - diagonal * yimag
        return (
            (wreal * mreal + wimag * mimag) * factor,
            (wimag * mreal - wreal * mimag) * factor,
        )

    greal = jnp.ones((tiles, 128), F32)
    gimag = jnp.zeros((tiles, 128), F32)

    def double_step(_, gains):
        first = single_step(*gains)
        fresh = single_step(*first)
        return tuple((a + b) * 0.5 for a, b in zip(fresh, first))

    greal, gimag = lax.fori_loop(0, ITERS // 2, double_step, (greal, gimag))
    wide_ref[0:128, :] = jnp.zeros((128, 128), F32)
    wide_ref[0:8, :] = greal[0:OWNED, :]
    wide_ref[8:16, :] = gimag[0:OWNED, :]
    out_ref[...] = wide_ref[0:128, :].T


def solve(ownr, owni, other, mreal, mimag, inverse):
    tiles = 2 * OWNED
    return pl.pallas_call(
        solve_kernel,
        out_shape=jax.ShapeDtypeStruct((128, 128), F32),
        scratch_shapes=[
            pltpu.VMEM((512, 128), F32),
            pltpu.VMEM((OWNED, SPECTRA, 128), F32),
            pltpu.VMEM((OWNED, SPECTRA, 128), F32),
            pltpu.VMEM((2, tiles, 128), F32),
            pltpu.VMEM((2, tiles * 8, 128), F32),
        ],
        compiler_params=pltpu.CompilerParams(vmem_limit_bytes=8 * 2**20),
        name="solve",
    )(ownr, owni, other, mreal, mimag, inverse)


ROWS = 128


def power_kernel(own_ref, other_ref, out_ref, wide_ref, line_ref, upper_ref, lower_ref, right_ref):
    half = lax.axis_index("bl")
    step = pl.program_id(0)

    @pl.when(step == 0)
    def _():
        for side, source in ((0, own_ref), (1, other_ref)):
            tile = half if side == 0 else 1 - half
            wide_ref[...] = source[...].astype(F32)
            for group in range(2):
                real = wide_ref[pl.ds(group, 128, 4), :]
                imag = wide_ref[pl.ds(2 + group, 128, 4), :]
                for j in range(4):
                    a = real[:, j * 32 : j * 32 + 32]
                    b = imag[:, j * 32 : j * 32 + 32]
                    line_ref[pl.ds(group * 4 + j, 128, OWNED), :] = jnp.concatenate(
                        [a, b, b, -a], axis=1
                    )
            lines = line_ref[...]
            start = pl.multiple_of(tile * 1024, 1024)
            right_ref[pl.ds(start, 1024), :] = lines[:, 0:64].astype(BF16)
            if side == 0:
                scaled = lines * (1.0 / SPECTRA)
                upper_ref[...] = scaled[:, 0:64].astype(BF16)
                lower_ref[...] = scaled[:, 64:128].astype(BF16)

    rows = pl.ds(pl.multiple_of(step * ROWS, ROWS), ROWS)
    for part, left in ((0, upper_ref), (1, lower_ref)):
        out_ref[part] = lax.dot_general(
            left[rows, :], right_ref[...], (((1,), (1,)), ((), ())),
            preferred_element_type=F32,
        ).astype(BF16)


def power(own, other):
    return pl.pallas_call(
        power_kernel,
        grid=(1024 // ROWS,),
        in_specs=[pl.BlockSpec((512, 128), lambda s: (0, 0))] * 2,
        out_specs=pl.BlockSpec((2, ROWS, 2048), lambda s: (0, s, 0)),
        out_shape=jax.ShapeDtypeStruct((2, 1024, 2048), BF16),
        scratch_shapes=[
            pltpu.VMEM((512, 128), F32),
            pltpu.VMEM((1024, 128), F32),
            pltpu.VMEM((1024, 64), BF16),
            pltpu.VMEM((1024, 64), BF16),
            pltpu.VMEM((2048, 64), BF16),
        ],
        compiler_params=pltpu.CompilerParams(vmem_limit_bytes=24 * 2**20),
        cost_estimate=pl.CostEstimate(
            flops=2 * 2 * 1024 * 2048 * 64, bytes_accessed=9 * 2**20, transcendentals=0
        ),
        name="power",
    )(own, other)


def turn_kernel(gains_ref, out_ref):
    turned = gains_ref[...].T
    out_ref[0, 0] = turned[0:8, :]
    out_ref[1, 0] = turned[8:16, :]


def on_device(voltages, model_magnitude, model_phase):
    half = lax.axis_index("bl")
    spectra = channelize(voltages[0])
    own = lax.all_to_all(spectra.reshape(CHANNELS, 4, 128), "gx", 0, 0)

    def tiles(values):
        halves = values.reshape(2, 128, OWNED).transpose(0, 2, 1)
        flipped = jnp.concatenate([halves[1:], halves[:1]], axis=0)
        return jnp.where(half == 0, halves, flipped).reshape(2 * OWNED, 128)

    magnitude, phase = tiles(model_magnitude), tiles(model_phase)
    mreal = magnitude * jnp.cos(phase)
    mimag = magnitude * jnp.sin(phase)
    inverse = 1.0 / (magnitude * magnitude)
    own, mreal, mimag, inverse = lax.optimization_barrier((own, mreal, mimag, inverse))
    own = own.reshape(512, 128)
    other = lax.ppermute(own, "bl", [(0, 1), (1, 0)])
    ownr, owni = own_turn(own)
    gains = solve(ownr, owni, other, mreal, mimag, inverse)
    moved = lax.all_to_all(gains.reshape(128, 1, 128), "gx", 0, 0)
    visible = power(own, other)
    gain_output = pl.pallas_call(
        turn_kernel,
        out_shape=jax.ShapeDtypeStruct((2, 1, OWNED, CHANNELS), F32),
        compiler_params=pltpu.CompilerParams(vmem_limit_bytes=2 * 2**20),
        name="turn",
    )(moved.reshape(128, 128))
    return visible[None], gain_output


def solution(mesh):
    in_specs = (P("bl", "gx", None), P("gx", None), P("gx", None))
    out_specs = (P("gx", None, "bl", None), P(None, "bl", "gx", None))
    return jax.shard_map(
        on_device, mesh=mesh, in_specs=in_specs, out_specs=out_specs, check_vma=False
    )
```

```python
import functools
import math

import jax
import jax.numpy as jnp
import numpy as np
from jax import lax
from jax.experimental import pallas as pl
from jax.experimental.pallas import tpu as pltpu
from jax.sharding import PartitionSpec as P

NFFT = 2048
TAPS = 4
SPECTRA = 32
ITERS = 4
CHANNELS = 128
OWNED = 8
EPSILON = 1e-06
F32 = jnp.float32
BF16 = jnp.bfloat16
FOLD = 256
FOLDS = NFFT // FOLD


def split_bf16(values):
    high = values.astype(np.float32).astype(jnp.bfloat16)
    low = (values - high.astype(np.float64)).astype(np.float32).astype(jnp.bfloat16)
    return high, low


def fold_weights():
    position = np.arange(TAPS * NFFT, dtype=np.float64) + 0.5
    hann = 0.5 - 0.5 * np.cos(2.0 * np.pi * position / (TAPS * NFFT))
    taper = np.sinc(position / NFFT - TAPS / 2.0) * hann
    taper = taper.reshape(TAPS, FOLDS, FOLD)
    signs = (-1.0) ** np.arange(FOLDS)
    folded = (taper * signs[None, :, None]).transpose(1, 0, 2)
    return folded.astype(np.float32)


def transform_weights():
    odd = 2 * np.arange(CHANNELS) + 1
    phase = (odd[:, None] * np.arange(FOLD)[None, :]) % (2 * FOLD)
    angle = phase.astype(np.float64) * (2.0 * np.pi / (2 * FOLD))
    scale = 1.0 / math.sqrt(NFFT)
    table = np.concatenate([np.cos(angle), -np.sin(angle)], axis=0) * scale
    high, low = split_bf16(table)
    return np.concatenate([high, low], axis=1)


GROUP = 8
GROUPS = SPECTRA // GROUP


def channelize_kernel(
    volts_hbm, window_hbm, table_hbm, out_ref,
    volts_ref, window_ref, table_ref, folded_ref, rows_ref, sems,
):
    def frames_copy(group):
        first = 0 if group == 0 else group * GROUP + TAPS - 1
        last = (group + 1) * GROUP + TAPS - 1
        span = pl.ds(first * NFFT, (last - first) * NFFT)
        return pltpu.make_async_copy(
            volts_hbm.at[:, span], volts_ref.at[:, span], sems.at[group]
        )

    window_copy = pltpu.make_async_copy(window_hbm, window_ref, sems.at[GROUPS])
    table_copy = pltpu.make_async_copy(table_hbm, table_ref, sems.at[GROUPS + 1])
    window_copy.start()
    for group in range(GROUPS):
        frames_copy(group).start()
    table_copy.start()
    window_copy.wait()
    for group in range(GROUPS):
        frames_copy(group).wait()
        for part in range(FOLD // 128):

            def fold_step(fold, sums):
                start = pl.multiple_of(fold * FOLD + part * 128, 128)
                taps = [
                    jnp.broadcast_to(
                        window_ref[fold, tap : tap + 1, part * 128 : part * 128 + 128],
                        (OWNED, 128),
                    )
                    for tap in range(TAPS)
                ]
                sums = list(sums)
                for frame in range(GROUP + TAPS - 1):
                    offset = start + (group * GROUP + frame) * NFFT
                    piece = volts_ref[:, pl.ds(offset, 128)].astype(F32)
                    for tap in range(TAPS):
                        s = frame - tap
                        if 0 <= s < GROUP:
                            sums[s] = sums[s] + piece * taps[tap]
                return tuple(sums)

            zero = jnp.zeros((OWNED, 128), F32)
            sums = lax.fori_loop(0, FOLDS, fold_step, (zero,) * GROUP, unroll=2)
            for s in range(GROUP):
                folded_ref[part, pl.ds((group * GROUP + s) * OWNED, OWNED), :] = sums[s]
    pieces = []
    for part in range(FOLD // 128):
        pieces.append(
            jnp.concatenate(
                [folded_ref[part, pl.ds(j, SPECTRA, OWNED), :] for j in range(OWNED)],
                axis=0,
            )
        )
    folded = jnp.concatenate(pieces, axis=1)
    high = folded.astype(BF16)
    low = (folded - high.astype(F32)).astype(BF16)
    table_copy.wait()
    across = (((1,), (1,)), ((), ()))
    spectra = (
        lax.dot_general(table_ref[:, 0:FOLD], high, across, preferred_element_type=F32)
        + lax.dot_general(table_ref[:, 0:FOLD], low, across, preferred_element_type=F32)
        + lax.dot_general(
            table_ref[:, FOLD : 2 * FOLD], high, across, preferred_element_type=F32
        )
    )
    for part in range(2):
        for side in range(2):
            rows_ref[pl.ds(part * 2 + side, CHANNELS, 4), :] = spectra[
                part * CHANNELS : (part + 1) * CHANNELS, side * 128 : side * 128 + 128
            ]
    out_ref[...] = rows_ref[...].astype(BF16)


def channelize(volts):
    return pl.pallas_call(
        channelize_kernel,
        out_shape=pltpu.VMEM((CHANNELS * 4, 128), BF16),
        in_specs=[pl.BlockSpec(memory_space=pltpu.HBM)] * 3,
        scratch_shapes=[
            pltpu.VMEM(volts.shape, BF16),
            pltpu.VMEM((FOLDS, TAPS, FOLD), F32),
            pltpu.VMEM((2 * CHANNELS, 2 * FOLD), BF16),
            pltpu.VMEM((2, SPECTRA * OWNED, 128), F32),
            pltpu.VMEM((CHANNELS * 4, 128), F32),
            pltpu.SemaphoreType.DMA((GROUPS + 2,)),
        ],
        compiler_params=pltpu.CompilerParams(vmem_limit_bytes=8 * 2**20),
        name="channelize",
    )(*[
        pltpu.with_memory_space_constraint(operand, pltpu.HBM)
        for operand in (
            volts, jnp.asarray(fold_weights()), jnp.asarray(transform_weights())
        )
    ])


def turn_spectra(source, wide_ref, real_ref, imag_ref):
    wide_ref[...] = source[...].astype(F32)
    for part, target in ((0, real_ref), (1, imag_ref)):
        for group in range(2):
            block = wide_ref[pl.ds(part * 2 + group, 128, 4), :].T
            for j in range(4):
                target[group * 4 + j] = block[j * 32 : j * 32 + 32, :]


def own_kernel(own_ref, real_ref, imag_ref, wide_ref):
    turn_spectra(own_ref, wide_ref, real_ref, imag_ref)


def own_turn(own):
    return pl.pallas_call(
        own_kernel,
        out_shape=[jax.ShapeDtypeStruct((OWNED, SPECTRA, 128), F32)] * 2,
        scratch_shapes=[pltpu.VMEM((512, 128), F32)],
        compiler_params=pltpu.CompilerParams(vmem_limit_bytes=4 * 2**20),
        cost_estimate=pl.CostEstimate(
            flops=2**22, bytes_accessed=2**20, transcendentals=0
        ),
        name="own_turn",
    )(own)


def solve_kernel(
    ownr_ref, owni_ref, other_ref, mreal_ref, mimag_ref, inverse_ref, out_ref,
    wide_ref, otherr_ref, otheri_ref, probe_ref, part_ref,
):
    turn_spectra(other_ref, wide_ref, otherr_ref, otheri_ref)
    tiles = 2 * OWNED

    def spectra_of(tile):
        if tile < OWNED:
            return ownr_ref[tile], owni_ref[tile]
        return otherr_ref[tile - OWNED], otheri_ref[tile - OWNED]

    def gathered(which):
        total = part_ref[which, pl.ds(0, tiles, 8), :]
        for row in range(1, 8):
            total = total + part_ref[which, pl.ds(row, tiles, 8), :]
        return total

    def eight(values):
        return (values[0:8] + values[8:16]) + (values[16:24] + values[24:32])

    for tile in range(tiles):
        real, imag = spectra_of(tile)
        part_ref[0, tile * 8 : tile * 8 + 8, :] = eight(real * real + imag * imag)
    diagonal = gathered(0) * (1.0 / SPECTRA)
    mreal, mimag, inverse = mreal_ref[...], mimag_ref[...], inverse_ref[...]

    def single_step(greal, gimag):
        yreal = greal * mreal - gimag * mimag
        yimag = greal * mimag + gimag * mreal
        energy = jnp.sum(yreal * yreal + yimag * yimag, keepdims=True) + EPSILON
        factor = inverse / energy
        probe_ref[0] = yreal
        probe_ref[1] = yimag
        areal = jnp.zeros((SPECTRA, 128), F32)
        aimag = jnp.zeros((SPECTRA, 128), F32)
        for tile in range(tiles):
            real, imag = spectra_of(tile)
            pr = jnp.broadcast_to(probe_ref[0, tile : tile + 1, :], (SPECTRA, 128))
            pi = jnp.broadcast_to(probe_ref[1, tile : tile + 1, :], (SPECTRA, 128))
            areal = areal + (real * pr + imag * pi)
            aimag = aimag + (real * pi - imag * pr)
        sreal = jnp.broadcast_to(jnp.sum(areal, axis=1, keepdims=True), (SPECTRA, 128))
        simag = jnp.broadcast_to(jnp.sum(aimag, axis=1, keepdims=True), (SPECTRA, 128))
        for tile in range(tiles):
            real, imag = spectra_of(tile)
            rows = slice(tile * 8, tile * 8 + 8)
            part_ref[0, rows, :] = eight(real * sreal - imag * simag)
            part_ref[1, rows, :] = eight(real * simag + imag * sreal)
        wreal = gathered(0) * (1.0 / SPECTRA) - diagonal * yreal
        wimag = gathered(1) * (1.0 / SPECTRA) - diagonal * yimag
        return (
            (wreal * mreal + wimag * mimag) * factor,
            (wimag * mreal - wreal * mimag) * factor,
        )

    greal = jnp.ones((tiles, 128), F32)
    gimag = jnp.zeros((tiles, 128), F32)

    def double_step(_, gains):
        first = single_step(*gains)
        fresh = single_step(*first)
        return tuple((a + b) * 0.5 for a, b in zip(fresh, first))

    greal, gimag = lax.fori_loop(0, ITERS // 2, double_step, (greal, gimag))
    wide_ref[0:128, :] = jnp.zeros((128, 128), F32)
    wide_ref[0:8, :] = greal[0:OWNED, :]
    wide_ref[8:16, :] = gimag[0:OWNED, :]
    out_ref[...] = wide_ref[0:128, :].T


def solve(ownr, owni, other, mreal, mimag, inverse):
    tiles = 2 * OWNED
    return pl.pallas_call(
        solve_kernel,
        out_shape=pltpu.VMEM((128, 128), F32),
        scratch_shapes=[
            pltpu.VMEM((512, 128), F32),
            pltpu.VMEM((OWNED, SPECTRA, 128), F32),
            pltpu.VMEM((OWNED, SPECTRA, 128), F32),
            pltpu.VMEM((2, tiles, 128), F32),
            pltpu.VMEM((2, tiles * 8, 128), F32),
        ],
        compiler_params=pltpu.CompilerParams(vmem_limit_bytes=8 * 2**20),
        name="solve",
    )(ownr, owni, other, mreal, mimag, inverse)


ROWS = 128


def power_kernel(own_ref, other_ref, out_ref, wide_ref, line_ref, upper_ref, lower_ref, right_ref):
    half = lax.axis_index("bl")
    step = pl.program_id(0)

    @pl.when(step == 0)
    def _():
        for side, source in ((0, own_ref), (1, other_ref)):
            tile = half if side == 0 else 1 - half
            wide_ref[...] = source[...].astype(F32)
            for group in range(2):
                real = wide_ref[pl.ds(group, 128, 4), :]
                imag = wide_ref[pl.ds(2 + group, 128, 4), :]
                for j in range(4):
                    a = real[:, j * 32 : j * 32 + 32]
                    b = imag[:, j * 32 : j * 32 + 32]
                    line_ref[pl.ds(group * 4 + j, 128, OWNED), :] = jnp.concatenate(
                        [a, b, b, -a], axis=1
                    )
            lines = line_ref[...]
            start = pl.multiple_of(tile * 1024, 1024)
            right_ref[pl.ds(start, 1024), :] = lines[:, 0:64].astype(BF16)
            if side == 0:
                scaled = lines * (1.0 / SPECTRA)
                upper_ref[...] = scaled[:, 0:64].astype(BF16)
                lower_ref[...] = scaled[:, 64:128].astype(BF16)

    rows = pl.ds(pl.multiple_of(step * ROWS, ROWS), ROWS)
    for part, left in ((0, upper_ref), (1, lower_ref)):
        out_ref[part] = lax.dot_general(
            left[rows, :], right_ref[...], (((1,), (1,)), ((), ())),
            preferred_element_type=F32,
        ).astype(BF16)


def power(own, other):
    return pl.pallas_call(
        power_kernel,
        grid=(1024 // ROWS,),
        in_specs=[pl.BlockSpec((512, 128), lambda s: (0, 0))] * 2,
        out_specs=pl.BlockSpec((2, ROWS, 2048), lambda s: (0, s, 0)),
        out_shape=jax.ShapeDtypeStruct((2, 1024, 2048), BF16),
        scratch_shapes=[
            pltpu.VMEM((512, 128), F32),
            pltpu.VMEM((1024, 128), F32),
            pltpu.VMEM((1024, 64), BF16),
            pltpu.VMEM((1024, 64), BF16),
            pltpu.VMEM((2048, 64), BF16),
        ],
        compiler_params=pltpu.CompilerParams(vmem_limit_bytes=24 * 2**20),
        cost_estimate=pl.CostEstimate(
            flops=2 * 2 * 1024 * 2048 * 64, bytes_accessed=9 * 2**20, transcendentals=0
        ),
        name="power",
    )(own, other)


def turn_kernel(gains_ref, out_ref):
    turned = gains_ref[...].T
    out_ref[0, 0] = turned[0:8, :]
    out_ref[1, 0] = turned[8:16, :]


def on_device(voltages, model_magnitude, model_phase):
    half = lax.axis_index("bl")
    spectra = channelize(voltages[0])
    own = lax.all_to_all(spectra.reshape(CHANNELS, 4, 128), "gx", 0, 0)

    def tiles(values):
        halves = values.reshape(2, 128, OWNED).transpose(0, 2, 1)
        flipped = jnp.concatenate([halves[1:], halves[:1]], axis=0)
        return jnp.where(half == 0, halves, flipped).reshape(2 * OWNED, 128)

    magnitude, phase = tiles(model_magnitude), tiles(model_phase)
    mreal = magnitude * jnp.cos(phase)
    mimag = magnitude * jnp.sin(phase)
    inverse = 1.0 / (magnitude * magnitude)
    own, mreal, mimag, inverse = lax.optimization_barrier((own, mreal, mimag, inverse))
    own = own.reshape(512, 128)
    other = lax.ppermute(own, "bl", [(0, 1), (1, 0)])
    ownr, owni = own_turn(own)
    gains = solve(ownr, owni, other, mreal, mimag, inverse)
    moved = lax.all_to_all(gains.reshape(128, 1, 128), "gx", 0, 0)
    visible = power(own, other)
    gain_output = pl.pallas_call(
        turn_kernel,
        out_shape=jax.ShapeDtypeStruct((2, 1, OWNED, CHANNELS), F32),
        compiler_params=pltpu.CompilerParams(vmem_limit_bytes=2 * 2**20),
        name="turn",
    )(moved.reshape(128, 128))
    return visible[None], gain_output


def solution(mesh):
    in_specs = (P("bl", "gx", None), P("gx", None), P("gx", None))
    out_specs = (P("gx", None, "bl", None), P(None, "bl", "gx", None))
    return jax.shard_map(
        on_device, mesh=mesh, in_specs=in_specs, out_specs=out_specs, check_vma=False
    )
```

```python
import functools
import math

import jax
import jax.numpy as jnp
import numpy as np
from jax import lax
from jax.experimental import pallas as pl
from jax.experimental.pallas import tpu as pltpu
from jax.sharding import PartitionSpec as P

NFFT = 2048
TAPS = 4
SPECTRA = 32
ITERS = 4
CHANNELS = 128
OWNED = 8
EPSILON = 1e-06
F32 = jnp.float32
BF16 = jnp.bfloat16
FOLD = 256
FOLDS = NFFT // FOLD


def split_bf16(values):
    high = values.astype(np.float32).astype(jnp.bfloat16)
    low = (values - high.astype(np.float64)).astype(np.float32).astype(jnp.bfloat16)
    return high, low


def fold_weights():
    position = np.arange(TAPS * NFFT, dtype=np.float64) + 0.5
    hann = 0.5 - 0.5 * np.cos(2.0 * np.pi * position / (TAPS * NFFT))
    taper = np.sinc(position / NFFT - TAPS / 2.0) * hann
    taper = taper.reshape(TAPS, FOLDS, FOLD)
    signs = (-1.0) ** np.arange(FOLDS)
    folded = (taper * signs[None, :, None]).transpose(1, 0, 2)
    return folded.astype(np.float32)


def transform_weights():
    odd = 2 * np.arange(CHANNELS) + 1
    phase = (odd[:, None] * np.arange(FOLD)[None, :]) % (2 * FOLD)
    angle = phase.astype(np.float64) * (2.0 * np.pi / (2 * FOLD))
    scale = 1.0 / math.sqrt(NFFT)
    table = np.concatenate([np.cos(angle), -np.sin(angle)], axis=0) * scale
    high, low = split_bf16(table)
    return np.concatenate([high, low], axis=1)


GROUP = 8
GROUPS = SPECTRA // GROUP
TILES = 2 * OWNED


def channelize_kernel(
    volts_hbm, window_hbm, table_hbm, magnitude_hbm, phase_hbm, out_ref, model_ref,
    volts_ref, window_ref, table_ref, magnitude_ref, phase_ref, folded_ref, rows_ref, sems,
):
    def frames_copy(first, count, slot):
        start = first * NFFT
        if not isinstance(first, int):
            start = pl.multiple_of(start, NFFT)
        span = pl.ds(start, count * NFFT)
        return pltpu.make_async_copy(
            volts_hbm.at[:, span], volts_ref.at[:, span], sems.at[slot]
        )

    lead = TAPS - 1
    copies = [
        pltpu.make_async_copy(window_hbm, window_ref, sems.at[GROUPS]),
        frames_copy(0, lead, GROUPS + 1),
    ]
    model_copies = [
        pltpu.make_async_copy(magnitude_hbm, magnitude_ref, sems.at[GROUPS + 2]),
        pltpu.make_async_copy(phase_hbm, phase_ref, sems.at[GROUPS + 3]),
    ]
    table_copy = pltpu.make_async_copy(table_hbm, table_ref, sems.at[GROUPS + 4])
    for copy in model_copies + copies:
        copy.start()
    for group in range(GROUPS):
        frames_copy(group * GROUP + lead, GROUP, group).start()
    table_copy.start()
    for copy in model_copies:
        copy.wait()
    magnitude, phase = magnitude_ref[...], phase_ref[...]
    model_ref[0:TILES, :] = magnitude * jnp.cos(phase)
    model_ref[TILES : 2 * TILES, :] = magnitude * jnp.sin(phase)
    model_ref[2 * TILES : 3 * TILES, :] = 1.0 / (magnitude * magnitude)
    for copy in copies:
        copy.wait()

    def group_step(group, carry):
        first = group * GROUP
        frames_copy(first + lead, GROUP, group).wait()
        for part in range(FOLD // 128):
            lanes = slice(part * 128, part * 128 + 128)
            sums = [jnp.zeros((OWNED, 128), F32)] * GROUP
            for fold in range(FOLDS):
                taps = [
                    jnp.broadcast_to(window_ref[fold, tap : tap + 1, lanes], (OWNED, 128))
                    for tap in range(TAPS)
                ]
                for frame in range(GROUP + TAPS - 1):
                    offset = (first + frame) * NFFT + fold * FOLD + part * 128
                    piece = volts_ref[:, pl.ds(pl.multiple_of(offset, 128), 128)]
                    piece = piece.astype(F32)
                    for tap in range(TAPS):
                        s = frame - tap
                        if 0 <= s < GROUP:
                            sums[s] = sums[s] + piece * taps[tap]
            for s in range(GROUP):
                row = pl.multiple_of((first + s) * OWNED, OWNED)
                folded_ref[part, pl.ds(row, OWNED), :] = sums[s]
        return carry

    lax.fori_loop(0, GROUPS, group_step, 0)
    pieces = []
    for part in range(FOLD // 128):
        pieces.append(
            jnp.concatenate(
                [folded_ref[part, pl.ds(j, SPECTRA, OWNED), :] for j in range(OWNED)],
                axis=0,
            )
        )
    folded = jnp.concatenate(pieces, axis=1)
    high = folded.astype(BF16)
    low = (folded - high.astype(F32)).astype(BF16)
    table_copy.wait()
    across = (((1,), (1,)), ((), ()))
    spectra = (
        lax.dot_general(table_ref[:, 0:FOLD], high, across, preferred_element_type=F32)
        + lax.dot_general(table_ref[:, 0:FOLD], low, across, preferred_element_type=F32)
        + lax.dot_general(
            table_ref[:, FOLD : 2 * FOLD], high, across, preferred_element_type=F32
        )
    )
    for part in range(2):
        for side in range(2):
            rows_ref[pl.ds(part * 2 + side, CHANNELS, 4), :] = spectra[
                part * CHANNELS : (part + 1) * CHANNELS, side * 128 : side * 128 + 128
            ]
    out_ref[...] = rows_ref[...].astype(BF16)


def channelize(volts, magnitude, phase):
    operands = (
        volts,
        jnp.asarray(fold_weights()),
        jnp.asarray(transform_weights()),
        magnitude.reshape(TILES, 128),
        phase.reshape(TILES, 128),
    )
    return pl.pallas_call(
        channelize_kernel,
        out_shape=[
            pltpu.VMEM((CHANNELS * 4, 128), BF16),
            pltpu.VMEM((3 * TILES, 128), F32),
        ],
        in_specs=[pl.BlockSpec(memory_space=pltpu.HBM)] * 5,
        scratch_shapes=[
            pltpu.VMEM(volts.shape, BF16),
            pltpu.VMEM((FOLDS, TAPS, FOLD), F32),
            pltpu.VMEM((2 * CHANNELS, 2 * FOLD), BF16),
            pltpu.VMEM((TILES, 128), F32),
            pltpu.VMEM((TILES, 128), F32),
            pltpu.VMEM((2, SPECTRA * OWNED, 128), F32),
            pltpu.VMEM((CHANNELS * 4, 128), F32),
            pltpu.SemaphoreType.DMA((GROUPS + 5,)),
        ],
        compiler_params=pltpu.CompilerParams(vmem_limit_bytes=8 * 2**20),
        name="channelize",
    )(*[pltpu.with_memory_space_constraint(x, pltpu.HBM) for x in operands])


def turn_spectra(source, wide_ref, real_ref, imag_ref):
    wide_ref[...] = source[...].astype(F32)
    for part, target in ((0, real_ref), (1, imag_ref)):
        for group in range(2):
            block = wide_ref[pl.ds(part * 2 + group, 128, 4), :].T
            for j in range(4):
                target[group * 4 + j] = block[j * 32 : j * 32 + 32, :]


def own_kernel(own_ref, real_ref, imag_ref, wide_ref):
    turn_spectra(own_ref, wide_ref, real_ref, imag_ref)


def own_turn(own):
    return pl.pallas_call(
        own_kernel,
        out_shape=[jax.ShapeDtypeStruct((OWNED, SPECTRA, 128), F32)] * 2,
        scratch_shapes=[pltpu.VMEM((512, 128), F32)],
        compiler_params=pltpu.CompilerParams(vmem_limit_bytes=4 * 2**20),
        cost_estimate=pl.CostEstimate(
            flops=2**22, bytes_accessed=2**20, transcendentals=0
        ),
        name="own_turn",
    )(own)


def solve_kernel(
    ownr_ref, owni_ref, other_ref, model_ref, out_ref,
    wide_ref, otherr_ref, otheri_ref, probe_ref, part_ref,
):
    turn_spectra(other_ref, wide_ref, otherr_ref, otheri_ref)
    tiles = 2 * OWNED

    def spectra_of(tile):
        if tile < OWNED:
            return ownr_ref[tile], owni_ref[tile]
        return otherr_ref[tile - OWNED], otheri_ref[tile - OWNED]

    def gathered(which):
        total = part_ref[which, pl.ds(0, tiles, 8), :]
        for row in range(1, 8):
            total = total + part_ref[which, pl.ds(row, tiles, 8), :]
        return total

    def eight(values):
        return (values[0:8] + values[8:16]) + (values[16:24] + values[24:32])

    for tile in range(tiles):
        real, imag = spectra_of(tile)
        part_ref[0, tile * 8 : tile * 8 + 8, :] = eight(real * real + imag * imag)
    diagonal = gathered(0) * (1.0 / SPECTRA)
    half = lax.axis_index("bl")

    def model(which):
        rows = [
            pl.ds(pl.multiple_of(which * tiles + side * OWNED, OWNED), OWNED)
            for side in (half, 1 - half)
        ]
        return jnp.concatenate([model_ref[r, :] for r in rows], axis=0)

    mreal, mimag, inverse = model(0), model(1), model(2)

    def single_step(greal, gimag):
        yreal = greal * mreal - gimag * mimag
        yimag = greal * mimag + gimag * mreal
        energy = jnp.sum(yreal * yreal + yimag * yimag, keepdims=True) + EPSILON
        factor = inverse / energy
        probe_ref[0] = yreal
        probe_ref[1] = yimag
        areal = jnp.zeros((SPECTRA, 128), F32)
        aimag = jnp.zeros((SPECTRA, 128), F32)
        for tile in range(tiles):
            real, imag = spectra_of(tile)
            pr = jnp.broadcast_to(probe_ref[0, tile : tile + 1, :], (SPECTRA, 128))
            pi = jnp.broadcast_to(probe_ref[1, tile : tile + 1, :], (SPECTRA, 128))
            areal = areal + (real * pr + imag * pi)
            aimag = aimag + (real * pi - imag * pr)
        sreal = jnp.broadcast_to(jnp.sum(areal, axis=1, keepdims=True), (SPECTRA, 128))
        simag = jnp.broadcast_to(jnp.sum(aimag, axis=1, keepdims=True), (SPECTRA, 128))
        for tile in range(tiles):
            real, imag = spectra_of(tile)
            rows = slice(tile * 8, tile * 8 + 8)
            part_ref[0, rows, :] = eight(real * sreal - imag * simag)
            part_ref[1, rows, :] = eight(real * simag + imag * sreal)
        wreal = gathered(0) * (1.0 / SPECTRA) - diagonal * yreal
        wimag = gathered(1) * (1.0 / SPECTRA) - diagonal * yimag
        return (
            (wreal * mreal + wimag * mimag) * factor,
            (wimag * mreal - wreal * mimag) * factor,
        )

    greal = jnp.ones((tiles, 128), F32)
    gimag = jnp.zeros((tiles, 128), F32)

    def double_step(_, gains):
        first = single_step(*gains)
        fresh = single_step(*first)
        return tuple((a + b) * 0.5 for a, b in zip(fresh, first))

    greal, gimag = lax.fori_loop(0, ITERS // 2, double_step, (greal, gimag))
    wide_ref[0:128, :] = jnp.zeros((128, 128), F32)
    wide_ref[0:8, :] = greal[0:OWNED, :]
    wide_ref[8:16, :] = gimag[0:OWNED, :]
    out_ref[...] = wide_ref[0:128, :].T


def solve(ownr, owni, other, model):
    tiles = 2 * OWNED
    return pl.pallas_call(
        solve_kernel,
        out_shape=pltpu.VMEM((128, 128), F32),
        scratch_shapes=[
            pltpu.VMEM((512, 128), F32),
            pltpu.VMEM((OWNED, SPECTRA, 128), F32),
            pltpu.VMEM((OWNED, SPECTRA, 128), F32),
            pltpu.VMEM((2, tiles, 128), F32),
            pltpu.VMEM((2, tiles * 8, 128), F32),
        ],
        compiler_params=pltpu.CompilerParams(vmem_limit_bytes=8 * 2**20),
        name="solve",
    )(ownr, owni, other, model)


ROWS = 128


def power_kernel(own_ref, other_ref, out_ref, wide_ref, line_ref, upper_ref, lower_ref, right_ref):
    half = lax.axis_index("bl")
    step = pl.program_id(0)

    @pl.when(step == 0)
    def _():
        for side, source in ((0, own_ref), (1, other_ref)):
            tile = half if side == 0 else 1 - half
            wide_ref[...] = source[...].astype(F32)
            for group in range(2):
                real = wide_ref[pl.ds(group, 128, 4), :]
                imag = wide_ref[pl.ds(2 + group, 128, 4), :]
                for j in range(4):
                    a = real[:, j * 32 : j * 32 + 32]
                    b = imag[:, j * 32 : j * 32 + 32]
                    line_ref[pl.ds(group * 4 + j, 128, OWNED), :] = jnp.concatenate(
                        [a, b, b, -a], axis=1
                    )
            lines = line_ref[...]
            start = pl.multiple_of(tile * 1024, 1024)
            right_ref[pl.ds(start, 1024), :] = lines[:, 0:64].astype(BF16)
            if side == 0:
                scaled = lines * (1.0 / SPECTRA)
                upper_ref[...] = scaled[:, 0:64].astype(BF16)
                lower_ref[...] = scaled[:, 64:128].astype(BF16)

    rows = pl.ds(pl.multiple_of(step * ROWS, ROWS), ROWS)
    for part, left in ((0, upper_ref), (1, lower_ref)):
        out_ref[part] = lax.dot_general(
            left[rows, :], right_ref[...], (((1,), (1,)), ((), ())),
            preferred_element_type=F32,
        ).astype(BF16)


def power(own, other):
    return pl.pallas_call(
        power_kernel,
        grid=(1024 // ROWS,),
        in_specs=[pl.BlockSpec((512, 128), lambda s: (0, 0))] * 2,
        out_specs=pl.BlockSpec((2, ROWS, 2048), lambda s: (0, s, 0)),
        out_shape=jax.ShapeDtypeStruct((2, 1024, 2048), BF16),
        scratch_shapes=[
            pltpu.VMEM((512, 128), F32),
            pltpu.VMEM((1024, 128), F32),
            pltpu.VMEM((1024, 64), BF16),
            pltpu.VMEM((1024, 64), BF16),
            pltpu.VMEM((2048, 64), BF16),
        ],
        compiler_params=pltpu.CompilerParams(vmem_limit_bytes=24 * 2**20),
        cost_estimate=pl.CostEstimate(
            flops=2 * 2 * 1024 * 2048 * 64, bytes_accessed=9 * 2**20, transcendentals=0
        ),
        name="power",
    )(own, other)


def turn_kernel(gains_ref, out_ref):
    turned = gains_ref[...].T
    out_ref[0, 0] = turned[0:8, :]
    out_ref[1, 0] = turned[8:16, :]


def on_device(voltages, model_magnitude, model_phase):
    spectra, model = channelize(voltages[0], model_magnitude, model_phase)
    own = lax.all_to_all(spectra.reshape(CHANNELS, 4, 128), "gx", 0, 0)
    own, model = lax.optimization_barrier((own, model))
    own = own.reshape(512, 128)
    other = lax.ppermute(own, "bl", [(0, 1), (1, 0)])
    model = model.reshape(6, 128, OWNED).transpose(0, 2, 1).reshape(3 * TILES, 128)
    ownr, owni = own_turn(own)
    gains = solve(ownr, owni, other, model)
    moved = lax.all_to_all(gains.reshape(128, 1, 128), "gx", 0, 0)
    visible = power(own, other)
    gain_output = pl.pallas_call(
        turn_kernel,
        out_shape=jax.ShapeDtypeStruct((2, 1, OWNED, CHANNELS), F32),
        compiler_params=pltpu.CompilerParams(vmem_limit_bytes=2 * 2**20),
        name="turn",
    )(moved.reshape(128, 128))
    return visible[None], gain_output


def solution(mesh):
    in_specs = (P("bl", "gx", None), P("gx", None), P("gx", None))
    out_specs = (P("gx", None, "bl", None), P(None, "bl", "gx", None))
    return jax.shard_map(
        on_device, mesh=mesh, in_specs=in_specs, out_specs=out_specs, check_vma=False
    )
```

```python
import functools
import math

import jax
import jax.numpy as jnp
import numpy as np
from jax import lax
from jax.experimental import pallas as pl
from jax.experimental.pallas import tpu as pltpu
from jax.sharding import PartitionSpec as P

NFFT = 2048
TAPS = 4
SPECTRA = 32
ITERS = 4
CHANNELS = 128
OWNED = 8
EPSILON = 1e-06
F32 = jnp.float32
BF16 = jnp.bfloat16
FOLD = 256
FOLDS = NFFT // FOLD


SIDE = 4
DEPTH = 8
PLANES = [
    [(x * DEPTH + z) * SIDE + y for x in range(SIDE) for y in range(SIDE)]
    for z in range(DEPTH)
]
LINES = [
    [(x * DEPTH + z) * SIDE + y for z in range(DEPTH)]
    for x in range(SIDE)
    for y in range(SIDE)
]


def split_bf16(values):
    high = values.astype(np.float32).astype(jnp.bfloat16)
    low = (values - high.astype(np.float64)).astype(np.float32).astype(jnp.bfloat16)
    return high, low


def fold_weights():
    position = np.arange(TAPS * NFFT, dtype=np.float64) + 0.5
    hann = 0.5 - 0.5 * np.cos(2.0 * np.pi * position / (TAPS * NFFT))
    taper = np.sinc(position / NFFT - TAPS / 2.0) * hann
    taper = taper.reshape(TAPS, FOLDS, FOLD)
    signs = (-1.0) ** np.arange(FOLDS)
    folded = (taper * signs[None, :, None]).transpose(1, 0, 2)
    return folded.astype(np.float32)


def transform_weights():
    odd = 2 * np.array(PLANES).T.reshape(CHANNELS) + 1
    phase = (odd[:, None] * np.arange(FOLD)[None, :]) % (2 * FOLD)
    angle = phase.astype(np.float64) * (2.0 * np.pi / (2 * FOLD))
    scale = 1.0 / math.sqrt(NFFT)
    table = np.concatenate([np.cos(angle), -np.sin(angle)], axis=0) * scale
    high, low = split_bf16(table)
    return np.concatenate([high, low], axis=1)


GROUP = 8
GROUPS = SPECTRA // GROUP
TILES = 2 * OWNED


def channelize_kernel(
    volts_hbm, window_hbm, table_hbm, magnitude_hbm, phase_hbm, out_ref, model_ref,
    volts_ref, window_ref, table_ref, magnitude_ref, phase_ref, folded_ref, rows_ref, sems,
):
    def frames_copy(first, count, slot):
        start = first * NFFT
        if not isinstance(first, int):
            start = pl.multiple_of(start, NFFT)
        span = pl.ds(start, count * NFFT)
        return pltpu.make_async_copy(
            volts_hbm.at[:, span], volts_ref.at[:, span], sems.at[slot]
        )

    lead = TAPS - 1
    copies = [
        pltpu.make_async_copy(window_hbm, window_ref, sems.at[GROUPS]),
        frames_copy(0, lead, GROUPS + 1),
    ]
    model_copies = [
        pltpu.make_async_copy(magnitude_hbm, magnitude_ref, sems.at[GROUPS + 2]),
        pltpu.make_async_copy(phase_hbm, phase_ref, sems.at[GROUPS + 3]),
    ]
    table_copy = pltpu.make_async_copy(table_hbm, table_ref, sems.at[GROUPS + 4])
    for copy in model_copies + copies:
        copy.start()
    for group in range(GROUPS):
        frames_copy(group * GROUP + lead, GROUP, group).start()
    table_copy.start()
    for copy in model_copies:
        copy.wait()
    magnitude, phase = magnitude_ref[...], phase_ref[...]
    model_ref[0:TILES, :] = magnitude * jnp.cos(phase)
    model_ref[TILES : 2 * TILES, :] = magnitude * jnp.sin(phase)
    model_ref[2 * TILES : 3 * TILES, :] = 1.0 / (magnitude * magnitude)
    for copy in copies:
        copy.wait()

    def group_step(group, carry):
        first = group * GROUP
        frames_copy(first + lead, GROUP, group).wait()
        for part in range(FOLD // 128):
            lanes = slice(part * 128, part * 128 + 128)
            sums = [jnp.zeros((OWNED, 128), F32)] * GROUP
            for fold in range(FOLDS):
                taps = [
                    jnp.broadcast_to(window_ref[fold, tap : tap + 1, lanes], (OWNED, 128))
                    for tap in range(TAPS)
                ]
                for frame in range(GROUP + TAPS - 1):
                    offset = (first + frame) * NFFT + fold * FOLD + part * 128
                    piece = volts_ref[:, pl.ds(pl.multiple_of(offset, 128), 128)]
                    piece = piece.astype(F32)
                    for tap in range(TAPS):
                        s = frame - tap
                        if 0 <= s < GROUP:
                            sums[s] = sums[s] + piece * taps[tap]
            for s in range(GROUP):
                row = pl.multiple_of((first + s) * OWNED, OWNED)
                folded_ref[part, pl.ds(row, OWNED), :] = sums[s]
        return carry

    lax.fori_loop(0, GROUPS, group_step, 0)
    pieces = []
    for part in range(FOLD // 128):
        pieces.append(
            jnp.concatenate(
                [folded_ref[part, pl.ds(j, SPECTRA, OWNED), :] for j in range(OWNED)],
                axis=0,
            )
        )
    folded = jnp.concatenate(pieces, axis=1)
    high = folded.astype(BF16)
    low = (folded - high.astype(F32)).astype(BF16)
    table_copy.wait()
    across = (((1,), (1,)), ((), ()))
    spectra = (
        lax.dot_general(table_ref[:, 0:FOLD], high, across, preferred_element_type=F32)
        + lax.dot_general(table_ref[:, 0:FOLD], low, across, preferred_element_type=F32)
        + lax.dot_general(
            table_ref[:, FOLD : 2 * FOLD], high, across, preferred_element_type=F32
        )
    )
    for part in range(2):
        for side in range(2):
            rows_ref[pl.ds(part * 2 + side, CHANNELS, 4), :] = spectra[
                part * CHANNELS : (part + 1) * CHANNELS, side * 128 : side * 128 + 128
            ]
    out_ref[...] = rows_ref[...].astype(BF16)


def channelize(volts, magnitude, phase):
    operands = (
        volts,
        jnp.asarray(fold_weights()),
        jnp.asarray(transform_weights()),
        magnitude.reshape(TILES, 128),
        phase.reshape(TILES, 128),
    )
    return pl.pallas_call(
        channelize_kernel,
        out_shape=[
            pltpu.VMEM((CHANNELS * 4, 128), BF16),
            pltpu.VMEM((3 * TILES, 128), F32),
        ],
        in_specs=[pl.BlockSpec(memory_space=pltpu.HBM)] * 5,
        scratch_shapes=[
            pltpu.VMEM(volts.shape, BF16),
            pltpu.VMEM((FOLDS, TAPS, FOLD), F32),
            pltpu.VMEM((2 * CHANNELS, 2 * FOLD), BF16),
            pltpu.VMEM((TILES, 128), F32),
            pltpu.VMEM((TILES, 128), F32),
            pltpu.VMEM((2, SPECTRA * OWNED, 128), F32),
            pltpu.VMEM((CHANNELS * 4, 128), F32),
            pltpu.SemaphoreType.DMA((GROUPS + 5,)),
        ],
        compiler_params=pltpu.CompilerParams(vmem_limit_bytes=8 * 2**20),
        name="channelize",
    )(*[pltpu.with_memory_space_constraint(x, pltpu.HBM) for x in operands])


def widen(source, wide_ref):
    for x in range(SIDE):
        for z in range(DEPTH):
            to, at = 16 * (x * DEPTH + z), 16 * (z * SIDE + x)
            wide_ref[to : to + 16, :] = source[at : at + 16, :].astype(F32)


def turn_spectra(source, wide_ref, real_ref, imag_ref):
    widen(source, wide_ref)
    for part, target in ((0, real_ref), (1, imag_ref)):
        for group in range(2):
            block = wide_ref[pl.ds(part * 2 + group, 128, 4), :].T
            for j in range(4):
                target[group * 4 + j] = block[j * 32 : j * 32 + 32, :]


def own_kernel(own_ref, real_ref, imag_ref, wide_ref):
    turn_spectra(own_ref, wide_ref, real_ref, imag_ref)


def own_turn(own):
    return pl.pallas_call(
        own_kernel,
        out_shape=[jax.ShapeDtypeStruct((OWNED, SPECTRA, 128), F32)] * 2,
        scratch_shapes=[pltpu.VMEM((512, 128), F32)],
        compiler_params=pltpu.CompilerParams(vmem_limit_bytes=4 * 2**20),
        cost_estimate=pl.CostEstimate(
            flops=2**22, bytes_accessed=2**20, transcendentals=0
        ),
        name="own_turn",
    )(own)


def solve_kernel(
    ownr_ref, owni_ref, other_ref, model_ref, out_ref,
    wide_ref, otherr_ref, otheri_ref, probe_ref, part_ref,
):
    turn_spectra(other_ref, wide_ref, otherr_ref, otheri_ref)
    tiles = 2 * OWNED

    def spectra_of(tile):
        if tile < OWNED:
            return ownr_ref[tile], owni_ref[tile]
        return otherr_ref[tile - OWNED], otheri_ref[tile - OWNED]

    def gathered(which):
        total = part_ref[which, pl.ds(0, tiles, 8), :]
        for row in range(1, 8):
            total = total + part_ref[which, pl.ds(row, tiles, 8), :]
        return total

    def eight(values):
        return (values[0:8] + values[8:16]) + (values[16:24] + values[24:32])

    for tile in range(tiles):
        real, imag = spectra_of(tile)
        part_ref[0, tile * 8 : tile * 8 + 8, :] = eight(real * real + imag * imag)
    diagonal = gathered(0) * (1.0 / SPECTRA)
    half = lax.axis_index("bl")

    def model(which):
        rows = [
            pl.ds(pl.multiple_of(which * tiles + side * OWNED, OWNED), OWNED)
            for side in (half, 1 - half)
        ]
        return jnp.concatenate([model_ref[r, :] for r in rows], axis=0)

    mreal, mimag, inverse = model(0), model(1), model(2)

    def single_step(greal, gimag):
        yreal = greal * mreal - gimag * mimag
        yimag = greal * mimag + gimag * mreal
        energy = jnp.sum(yreal * yreal + yimag * yimag, keepdims=True) + EPSILON
        factor = inverse / energy
        probe_ref[0] = yreal
        probe_ref[1] = yimag
        areal = jnp.zeros((SPECTRA, 128), F32)
        aimag = jnp.zeros((SPECTRA, 128), F32)
        for tile in range(tiles):
            real, imag = spectra_of(tile)
            pr = jnp.broadcast_to(probe_ref[0, tile : tile + 1, :], (SPECTRA, 128))
            pi = jnp.broadcast_to(probe_ref[1, tile : tile + 1, :], (SPECTRA, 128))
            areal = areal + (real * pr + imag * pi)
            aimag = aimag + (real * pi - imag * pr)
        sreal = jnp.broadcast_to(jnp.sum(areal, axis=1, keepdims=True), (SPECTRA, 128))
        simag = jnp.broadcast_to(jnp.sum(aimag, axis=1, keepdims=True), (SPECTRA, 128))
        for tile in range(tiles):
            real, imag = spectra_of(tile)
            rows = slice(tile * 8, tile * 8 + 8)
            part_ref[0, rows, :] = eight(real * sreal - imag * simag)
            part_ref[1, rows, :] = eight(real * simag + imag * sreal)
        wreal = gathered(0) * (1.0 / SPECTRA) - diagonal * yreal
        wimag = gathered(1) * (1.0 / SPECTRA) - diagonal * yimag
        return (
            (wreal * mreal + wimag * mimag) * factor,
            (wimag * mreal - wreal * mimag) * factor,
        )

    greal = jnp.ones((tiles, 128), F32)
    gimag = jnp.zeros((tiles, 128), F32)

    def double_step(_, gains):
        first = single_step(*gains)
        fresh = single_step(*first)
        return tuple((a + b) * 0.5 for a, b in zip(fresh, first))

    greal, gimag = lax.fori_loop(0, ITERS // 2, double_step, (greal, gimag))
    wide_ref[0:128, :] = jnp.zeros((128, 128), F32)
    wide_ref[0:8, :] = greal[0:OWNED, :]
    wide_ref[8:16, :] = gimag[0:OWNED, :]
    out_ref[...] = wide_ref[0:128, :].T


def solve(ownr, owni, other, model):
    tiles = 2 * OWNED
    return pl.pallas_call(
        solve_kernel,
        out_shape=pltpu.VMEM((128, 128), F32),
        scratch_shapes=[
            pltpu.VMEM((512, 128), F32),
            pltpu.VMEM((OWNED, SPECTRA, 128), F32),
            pltpu.VMEM((OWNED, SPECTRA, 128), F32),
            pltpu.VMEM((2, tiles, 128), F32),
            pltpu.VMEM((2, tiles * 8, 128), F32),
        ],
        compiler_params=pltpu.CompilerParams(vmem_limit_bytes=8 * 2**20),
        name="solve",
    )(ownr, owni, other, model)


ROWS = 128


def power_kernel(own_ref, other_ref, out_ref, wide_ref, line_ref, upper_ref, lower_ref, right_ref):
    half = lax.axis_index("bl")
    step = pl.program_id(0)

    @pl.when(step == 0)
    def _():
        for side, source in ((0, own_ref), (1, other_ref)):
            tile = half if side == 0 else 1 - half
            widen(source, wide_ref)
            for group in range(2):
                real = wide_ref[pl.ds(group, 128, 4), :]
                imag = wide_ref[pl.ds(2 + group, 128, 4), :]
                for j in range(4):
                    a = real[:, j * 32 : j * 32 + 32]
                    b = imag[:, j * 32 : j * 32 + 32]
                    line_ref[pl.ds(group * 4 + j, 128, OWNED), :] = jnp.concatenate(
                        [a, b, b, -a], axis=1
                    )
            lines = line_ref[...]
            start = pl.multiple_of(tile * 1024, 1024)
            right_ref[pl.ds(start, 1024), :] = lines[:, 0:64].astype(BF16)
            if side == 0:
                scaled = lines * (1.0 / SPECTRA)
                upper_ref[...] = scaled[:, 0:64].astype(BF16)
                lower_ref[...] = scaled[:, 64:128].astype(BF16)

    rows = pl.ds(pl.multiple_of(step * ROWS, ROWS), ROWS)
    for part, left in ((0, upper_ref), (1, lower_ref)):
        out_ref[part] = lax.dot_general(
            left[rows, :], right_ref[...], (((1,), (1,)), ((), ())),
            preferred_element_type=F32,
        ).astype(BF16)


def power(own, other):
    return pl.pallas_call(
        power_kernel,
        grid=(1024 // ROWS,),
        in_specs=[pl.BlockSpec((512, 128), lambda s: (0, 0))] * 2,
        out_specs=pl.BlockSpec((2, ROWS, 2048), lambda s: (0, s, 0)),
        out_shape=jax.ShapeDtypeStruct((2, 1024, 2048), BF16),
        scratch_shapes=[
            pltpu.VMEM((512, 128), F32),
            pltpu.VMEM((1024, 128), F32),
            pltpu.VMEM((1024, 64), BF16),
            pltpu.VMEM((1024, 64), BF16),
            pltpu.VMEM((2048, 64), BF16),
        ],
        compiler_params=pltpu.CompilerParams(vmem_limit_bytes=24 * 2**20),
        cost_estimate=pl.CostEstimate(
            flops=2 * 2 * 1024 * 2048 * 64, bytes_accessed=9 * 2**20, transcendentals=0
        ),
        name="power",
    )(own, other)


def turn_kernel(gains_ref, out_ref):
    turned = gains_ref[...].T
    out_ref[0, 0] = turned[0:8, :]
    out_ref[1, 0] = turned[8:16, :]


def on_device(voltages, model_magnitude, model_phase):
    spectra, model = channelize(voltages[0], model_magnitude, model_phase)
    staged = spectra.reshape(SIDE * SIDE, DEPTH, 4, 128)
    staged = lax.all_to_all(staged, "gx", 0, 0, axis_index_groups=PLANES)
    staged = staged.transpose(1, 0, 2, 3)
    own = lax.all_to_all(staged, "gx", 0, 0, axis_index_groups=LINES)
    own, model = lax.optimization_barrier((own, model))
    own = own.reshape(512, 128)
    other = lax.ppermute(own, "bl", [(0, 1), (1, 0)])
    model = model.reshape(6, 128, OWNED).transpose(0, 2, 1).reshape(3 * TILES, 128)
    ownr, owni = own_turn(own)
    gains = solve(ownr, owni, other, model)
    moved = lax.all_to_all(gains.reshape(128, 1, 128), "gx", 0, 0)
    visible = power(own, other)
    gain_output = pl.pallas_call(
        turn_kernel,
        out_shape=jax.ShapeDtypeStruct((2, 1, OWNED, CHANNELS), F32),
        compiler_params=pltpu.CompilerParams(vmem_limit_bytes=2 * 2**20),
        name="turn",
    )(moved.reshape(128, 128))
    return visible[None], gain_output


def solution(mesh):
    in_specs = (P("bl", "gx", None), P("gx", None), P("gx", None))
    out_specs = (P("gx", None, "bl", None), P(None, "bl", "gx", None))
    return jax.shard_map(
        on_device, mesh=mesh, in_specs=in_specs, out_specs=out_specs, check_vma=False
    )
```

```python
import functools
import math

import jax
import jax.numpy as jnp
import numpy as np
from jax import lax
from jax.experimental import pallas as pl
from jax.experimental.pallas import tpu as pltpu
from jax.sharding import PartitionSpec as P

NFFT = 2048
TAPS = 4
SPECTRA = 32
ITERS = 4
CHANNELS = 128
OWNED = 8
EPSILON = 1e-06
F32 = jnp.float32
BF16 = jnp.bfloat16
FOLD = 256
FOLDS = NFFT // FOLD


FIRST = (2 * 8 + 5) * 4 + 2
MEMBERS = list(range(CHANNELS))
MEMBERS[0], MEMBERS[FIRST] = FIRST, 0


def exchange(values):
    return lax.all_to_all(values, "gx", 0, 0, axis_index_groups=[MEMBERS])


def unswap(ref, rows):
    here, there = slice(0, rows), slice(FIRST * rows, (FIRST + 1) * rows)
    first, second = ref[here, :], ref[there, :]
    ref[here, :] = second
    ref[there, :] = first


def split_bf16(values):
    high = values.astype(np.float32).astype(jnp.bfloat16)
    low = (values - high.astype(np.float64)).astype(np.float32).astype(jnp.bfloat16)
    return high, low


def fold_weights():
    position = np.arange(TAPS * NFFT, dtype=np.float64) + 0.5
    hann = 0.5 - 0.5 * np.cos(2.0 * np.pi * position / (TAPS * NFFT))
    taper = np.sinc(position / NFFT - TAPS / 2.0) * hann
    taper = taper.reshape(TAPS, FOLDS, FOLD)
    signs = (-1.0) ** np.arange(FOLDS)
    folded = (taper * signs[None, :, None]).transpose(1, 0, 2)
    return folded.astype(np.float32)


def transform_weights():
    odd = 2 * np.array(MEMBERS) + 1
    phase = (odd[:, None] * np.arange(FOLD)[None, :]) % (2 * FOLD)
    angle = phase.astype(np.float64) * (2.0 * np.pi / (2 * FOLD))
    scale = 1.0 / math.sqrt(NFFT)
    table = np.concatenate([np.cos(angle), -np.sin(angle)], axis=0) * scale
    high, low = split_bf16(table)
    return np.concatenate([high, low], axis=1)


GROUP = 8
GROUPS = SPECTRA // GROUP
TILES = 2 * OWNED


def channelize_kernel(
    volts_hbm, window_hbm, table_hbm, magnitude_hbm, phase_hbm, out_ref, model_ref,
    volts_ref, window_ref, table_ref, magnitude_ref, phase_ref, folded_ref, rows_ref, sems,
):
    def frames_copy(first, count, slot):
        start = first * NFFT
        if not isinstance(first, int):
            start = pl.multiple_of(start, NFFT)
        span = pl.ds(start, count * NFFT)
        return pltpu.make_async_copy(
            volts_hbm.at[:, span], volts_ref.at[:, span], sems.at[slot]
        )

    lead = TAPS - 1
    copies = [
        pltpu.make_async_copy(window_hbm, window_ref, sems.at[GROUPS]),
        frames_copy(0, lead, GROUPS + 1),
    ]
    model_copies = [
        pltpu.make_async_copy(magnitude_hbm, magnitude_ref, sems.at[GROUPS + 2]),
        pltpu.make_async_copy(phase_hbm, phase_ref, sems.at[GROUPS + 3]),
    ]
    table_copy = pltpu.make_async_copy(table_hbm, table_ref, sems.at[GROUPS + 4])
    for copy in model_copies + copies:
        copy.start()
    for group in range(GROUPS):
        frames_copy(group * GROUP + lead, GROUP, group).start()
    table_copy.start()
    for copy in model_copies:
        copy.wait()
    magnitude, phase = magnitude_ref[...], phase_ref[...]
    model_ref[0:TILES, :] = magnitude * jnp.cos(phase)
    model_ref[TILES : 2 * TILES, :] = magnitude * jnp.sin(phase)
    model_ref[2 * TILES : 3 * TILES, :] = 1.0 / (magnitude * magnitude)
    for copy in copies:
        copy.wait()

    def group_step(group, carry):
        first = group * GROUP
        frames_copy(first + lead, GROUP, group).wait()
        for part in range(FOLD // 128):
            lanes = slice(part * 128, part * 128 + 128)
            sums = [jnp.zeros((OWNED, 128), F32)] * GROUP
            for fold in range(FOLDS):
                taps = [
                    jnp.broadcast_to(window_ref[fold, tap : tap + 1, lanes], (OWNED, 128))
                    for tap in range(TAPS)
                ]
                for frame in range(GROUP + TAPS - 1):
                    offset = (first + frame) * NFFT + fold * FOLD + part * 128
                    piece = volts_ref[:, pl.ds(pl.multiple_of(offset, 128), 128)]
                    piece = piece.astype(F32)
                    for tap in range(TAPS):
                        s = frame - tap
                        if 0 <= s < GROUP:
                            sums[s] = sums[s] + piece * taps[tap]
            for s in range(GROUP):
                row = pl.multiple_of((first + s) * OWNED, OWNED)
                folded_ref[part, pl.ds(row, OWNED), :] = sums[s]
        return carry

    lax.fori_loop(0, GROUPS, group_step, 0)
    pieces = []
    for part in range(FOLD // 128):
        pieces.append(
            jnp.concatenate(
                [folded_ref[part, pl.ds(j, SPECTRA, OWNED), :] for j in range(OWNED)],
                axis=0,
            )
        )
    folded = jnp.concatenate(pieces, axis=1)
    high = folded.astype(BF16)
    low = (folded - high.astype(F32)).astype(BF16)
    table_copy.wait()
    across = (((1,), (1,)), ((), ()))
    spectra = (
        lax.dot_general(table_ref[:, 0:FOLD], high, across, preferred_element_type=F32)
        + lax.dot_general(table_ref[:, 0:FOLD], low, across, preferred_element_type=F32)
        + lax.dot_general(
            table_ref[:, FOLD : 2 * FOLD], high, across, preferred_element_type=F32
        )
    )
    for part in range(2):
        for side in range(2):
            rows_ref[pl.ds(part * 2 + side, CHANNELS, 4), :] = spectra[
                part * CHANNELS : (part + 1) * CHANNELS, side * 128 : side * 128 + 128
            ]
    out_ref[...] = rows_ref[...].astype(BF16)


def channelize(volts, magnitude, phase):
    operands = (
        volts,
        jnp.asarray(fold_weights()),
        jnp.asarray(transform_weights()),
        magnitude.reshape(TILES, 128),
        phase.reshape(TILES, 128),
    )
    return pl.pallas_call(
        channelize_kernel,
        out_shape=[
            pltpu.VMEM((CHANNELS * 4, 128), BF16),
            pltpu.VMEM((3 * TILES, 128), F32),
        ],
        in_specs=[pl.BlockSpec(memory_space=pltpu.HBM)] * 5,
        scratch_shapes=[
            pltpu.VMEM(volts.shape, BF16),
            pltpu.VMEM((FOLDS, TAPS, FOLD), F32),
            pltpu.VMEM((2 * CHANNELS, 2 * FOLD), BF16),
            pltpu.VMEM((TILES, 128), F32),
            pltpu.VMEM((TILES, 128), F32),
            pltpu.VMEM((2, SPECTRA * OWNED, 128), F32),
            pltpu.VMEM((CHANNELS * 4, 128), F32),
            pltpu.SemaphoreType.DMA((GROUPS + 5,)),
        ],
        compiler_params=pltpu.CompilerParams(vmem_limit_bytes=8 * 2**20),
        name="channelize",
    )(*[pltpu.with_memory_space_constraint(x, pltpu.HBM) for x in operands])


def turn_spectra(source, wide_ref, real_ref, imag_ref):
    wide_ref[...] = source[...].astype(F32)
    unswap(wide_ref, 4)
    for part, target in ((0, real_ref), (1, imag_ref)):
        for group in range(2):
            block = wide_ref[pl.ds(part * 2 + group, 128, 4), :].T
            for j in range(4):
                target[group * 4 + j] = block[j * 32 : j * 32 + 32, :]


def own_kernel(own_ref, real_ref, imag_ref, wide_ref):
    turn_spectra(own_ref, wide_ref, real_ref, imag_ref)


def own_turn(own):
    return pl.pallas_call(
        own_kernel,
        out_shape=[jax.ShapeDtypeStruct((OWNED, SPECTRA, 128), F32)] * 2,
        scratch_shapes=[pltpu.VMEM((512, 128), F32)],
        compiler_params=pltpu.CompilerParams(vmem_limit_bytes=4 * 2**20),
        cost_estimate=pl.CostEstimate(
            flops=2**22, bytes_accessed=2**20, transcendentals=0
        ),
        name="own_turn",
    )(own)


def solve_kernel(
    ownr_ref, owni_ref, other_ref, model_ref, out_ref,
    wide_ref, otherr_ref, otheri_ref, probe_ref, part_ref,
):
    turn_spectra(other_ref, wide_ref, otherr_ref, otheri_ref)
    tiles = 2 * OWNED

    def spectra_of(tile):
        if tile < OWNED:
            return ownr_ref[tile], owni_ref[tile]
        return otherr_ref[tile - OWNED], otheri_ref[tile - OWNED]

    def gathered(which):
        total = part_ref[which, pl.ds(0, tiles, 8), :]
        for row in range(1, 8):
            total = total + part_ref[which, pl.ds(row, tiles, 8), :]
        return total

    def eight(values):
        return (values[0:8] + values[8:16]) + (values[16:24] + values[24:32])

    for tile in range(tiles):
        real, imag = spectra_of(tile)
        part_ref[0, tile * 8 : tile * 8 + 8, :] = eight(real * real + imag * imag)
    diagonal = gathered(0) * (1.0 / SPECTRA)
    half = lax.axis_index("bl")

    def model(which):
        rows = [
            pl.ds(pl.multiple_of(which * tiles + side * OWNED, OWNED), OWNED)
            for side in (half, 1 - half)
        ]
        return jnp.concatenate([model_ref[r, :] for r in rows], axis=0)

    mreal, mimag, inverse = model(0), model(1), model(2)

    def single_step(greal, gimag):
        yreal = greal * mreal - gimag * mimag
        yimag = greal * mimag + gimag * mreal
        energy = jnp.sum(yreal * yreal + yimag * yimag, keepdims=True) + EPSILON
        factor = inverse / energy
        probe_ref[0] = yreal
        probe_ref[1] = yimag
        areal = jnp.zeros((SPECTRA, 128), F32)
        aimag = jnp.zeros((SPECTRA, 128), F32)
        for tile in range(tiles):
            real, imag = spectra_of(tile)
            pr = jnp.broadcast_to(probe_ref[0, tile : tile + 1, :], (SPECTRA, 128))
            pi = jnp.broadcast_to(probe_ref[1, tile : tile + 1, :], (SPECTRA, 128))
            areal = areal + (real * pr + imag * pi)
            aimag = aimag + (real * pi - imag * pr)
        sreal = jnp.broadcast_to(jnp.sum(areal, axis=1, keepdims=True), (SPECTRA, 128))
        simag = jnp.broadcast_to(jnp.sum(aimag, axis=1, keepdims=True), (SPECTRA, 128))
        for tile in range(tiles):
            real, imag = spectra_of(tile)
            rows = slice(tile * 8, tile * 8 + 8)
            part_ref[0, rows, :] = eight(real * sreal - imag * simag)
            part_ref[1, rows, :] = eight(real * simag + imag * sreal)
        wreal = gathered(0) * (1.0 / SPECTRA) - diagonal * yreal
        wimag = gathered(1) * (1.0 / SPECTRA) - diagonal * yimag
        return (
            (wreal * mreal + wimag * mimag) * factor,
            (wimag * mreal - wreal * mimag) * factor,
        )

    greal = jnp.ones((tiles, 128), F32)
    gimag = jnp.zeros((tiles, 128), F32)

    def double_step(_, gains):
        first = single_step(*gains)
        fresh = single_step(*first)
        return tuple((a + b) * 0.5 for a, b in zip(fresh, first))

    greal, gimag = lax.fori_loop(0, ITERS // 2, double_step, (greal, gimag))
    wide_ref[0:128, :] = jnp.zeros((128, 128), F32)
    wide_ref[0:8, :] = greal[0:OWNED, :]
    wide_ref[8:16, :] = gimag[0:OWNED, :]
    out_ref[...] = wide_ref[0:128, :].T
    unswap(out_ref, 1)


def solve(ownr, owni, other, model):
    tiles = 2 * OWNED
    return pl.pallas_call(
        solve_kernel,
        out_shape=pltpu.VMEM((128, 128), F32),
        scratch_shapes=[
            pltpu.VMEM((512, 128), F32),
            pltpu.VMEM((OWNED, SPECTRA, 128), F32),
            pltpu.VMEM((OWNED, SPECTRA, 128), F32),
            pltpu.VMEM((2, tiles, 128), F32),
            pltpu.VMEM((2, tiles * 8, 128), F32),
        ],
        compiler_params=pltpu.CompilerParams(vmem_limit_bytes=8 * 2**20),
        name="solve",
    )(ownr, owni, other, model)


ROWS = 128


def power_kernel(own_ref, other_ref, out_ref, wide_ref, line_ref, upper_ref, lower_ref, right_ref):
    half = lax.axis_index("bl")
    step = pl.program_id(0)

    @pl.when(step == 0)
    def _():
        for side, source in ((0, own_ref), (1, other_ref)):
            tile = half if side == 0 else 1 - half
            wide_ref[...] = source[...].astype(F32)
            unswap(wide_ref, 4)
            for group in range(2):
                real = wide_ref[pl.ds(group, 128, 4), :]
                imag = wide_ref[pl.ds(2 + group, 128, 4), :]
                for j in range(4):
                    a = real[:, j * 32 : j * 32 + 32]
                    b = imag[:, j * 32 : j * 32 + 32]
                    line_ref[pl.ds(group * 4 + j, 128, OWNED), :] = jnp.concatenate(
                        [a, b, b, -a], axis=1
                    )
            lines = line_ref[...]
            start = pl.multiple_of(tile * 1024, 1024)
            right_ref[pl.ds(start, 1024), :] = lines[:, 0:64].astype(BF16)
            if side == 0:
                scaled = lines * (1.0 / SPECTRA)
                upper_ref[...] = scaled[:, 0:64].astype(BF16)
                lower_ref[...] = scaled[:, 64:128].astype(BF16)

    rows = pl.ds(pl.multiple_of(step * ROWS, ROWS), ROWS)
    for part, left in ((0, upper_ref), (1, lower_ref)):
        out_ref[part] = lax.dot_general(
            left[rows, :], right_ref[...], (((1,), (1,)), ((), ())),
            preferred_element_type=F32,
        ).astype(BF16)


def power(own, other):
    return pl.pallas_call(
        power_kernel,
        grid=(1024 // ROWS,),
        in_specs=[pl.BlockSpec((512, 128), lambda s: (0, 0))] * 2,
        out_specs=pl.BlockSpec((2, ROWS, 2048), lambda s: (0, s, 0)),
        out_shape=jax.ShapeDtypeStruct((2, 1024, 2048), BF16),
        scratch_shapes=[
            pltpu.VMEM((512, 128), F32),
            pltpu.VMEM((1024, 128), F32),
            pltpu.VMEM((1024, 64), BF16),
            pltpu.VMEM((1024, 64), BF16),
            pltpu.VMEM((2048, 64), BF16),
        ],
        compiler_params=pltpu.CompilerParams(vmem_limit_bytes=24 * 2**20),
        cost_estimate=pl.CostEstimate(
            flops=2 * 2 * 1024 * 2048 * 64, bytes_accessed=9 * 2**20, transcendentals=0
        ),
        name="power",
    )(own, other)


def turn_kernel(gains_ref, out_ref, rows_ref):
    rows_ref[...] = gains_ref[...]
    unswap(rows_ref, 1)
    turned = rows_ref[...].T
    out_ref[0, 0] = turned[0:8, :]
    out_ref[1, 0] = turned[8:16, :]


def on_device(voltages, model_magnitude, model_phase):
    spectra, model = channelize(voltages[0], model_magnitude, model_phase)
    own = exchange(spectra.reshape(CHANNELS, 4, 128))
    own, model = lax.optimization_barrier((own, model))
    own = own.reshape(512, 128)
    other = lax.ppermute(own, "bl", [(0, 1), (1, 0)])
    model = model.reshape(6, 128, OWNED).transpose(0, 2, 1).reshape(3 * TILES, 128)
    ownr, owni = own_turn(own)
    gains = solve(ownr, owni, other, model)
    moved = exchange(gains.reshape(128, 1, 128))
    visible = power(own, other)
    gain_output = pl.pallas_call(
        turn_kernel,
        out_shape=jax.ShapeDtypeStruct((2, 1, OWNED, CHANNELS), F32),
        scratch_shapes=[pltpu.VMEM((128, 128), F32)],
        compiler_params=pltpu.CompilerParams(vmem_limit_bytes=2 * 2**20),
        name="turn",
    )(moved.reshape(128, 128))
    return visible[None], gain_output


def solution(mesh):
    in_specs = (P("bl", "gx", None), P("gx", None), P("gx", None))
    out_specs = (P("gx", None, "bl", None), P(None, "bl", "gx", None))
    return jax.shard_map(
        on_device, mesh=mesh, in_specs=in_specs, out_specs=out_specs, check_vma=False
    )
```

```python
import functools
import math

import jax
import jax.numpy as jnp
import numpy as np
from jax import lax
from jax.experimental import pallas as pl
from jax.experimental.pallas import tpu as pltpu
from jax.sharding import PartitionSpec as P

NFFT = 2048
TAPS = 4
SPECTRA = 32
ITERS = 4
CHANNELS = 128
OWNED = 8
HALF = 1024
EPSILON = 1e-06
F32 = jnp.float32
BF16 = jnp.bfloat16
FOLD = 256
FOLDS = NFFT // FOLD


FIRST = (2 * 8 + 5) * 4 + 2
MEMBERS = list(range(CHANNELS))
MEMBERS[0], MEMBERS[FIRST] = FIRST, 0


def exchange(values):
    return lax.all_to_all(values, "gx", 0, 0, axis_index_groups=[MEMBERS])


def unswap(ref, rows):
    here, there = slice(0, rows), slice(FIRST * rows, (FIRST + 1) * rows)
    first, second = ref[here, :], ref[there, :]
    ref[here, :] = second
    ref[there, :] = first


def split_bf16(values):
    high = values.astype(np.float32).astype(jnp.bfloat16)
    low = (values - high.astype(np.float64)).astype(np.float32).astype(jnp.bfloat16)
    return high, low


def fold_weights():
    position = np.arange(TAPS * NFFT, dtype=np.float64) + 0.5
    hann = 0.5 - 0.5 * np.cos(2.0 * np.pi * position / (TAPS * NFFT))
    taper = np.sinc(position / NFFT - TAPS / 2.0) * hann
    taper = taper.reshape(TAPS, FOLDS, FOLD)
    signs = (-1.0) ** np.arange(FOLDS)
    folded = (taper * signs[None, :, None]).transpose(1, 0, 2)
    return folded.astype(np.float32)


def transform_weights():
    odd = 2 * np.array(MEMBERS) + 1
    phase = (odd[:, None] * np.arange(FOLD)[None, :]) % (2 * FOLD)
    angle = phase.astype(np.float64) * (2.0 * np.pi / (2 * FOLD))
    scale = 1.0 / math.sqrt(NFFT)
    table = np.concatenate([np.cos(angle), -np.sin(angle)], axis=0) * scale
    high, low = split_bf16(table)
    return np.concatenate([high, low], axis=1)


GROUP = 8
GROUPS = SPECTRA // GROUP
TILES = 2 * OWNED


def channelize_kernel(
    volts_hbm, window_hbm, table_hbm, magnitude_hbm, phase_hbm, out_ref, model_ref,
    volts_ref, window_ref, table_ref, magnitude_ref, phase_ref, folded_ref, rows_ref, sems,
):
    def frames_copy(first, count, slot):
        start = first * NFFT
        if not isinstance(first, int):
            start = pl.multiple_of(start, NFFT)
        span = pl.ds(start, count * NFFT)
        return pltpu.make_async_copy(
            volts_hbm.at[:, span], volts_ref.at[:, span], sems.at[slot]
        )

    lead = TAPS - 1
    copies = [
        pltpu.make_async_copy(window_hbm, window_ref, sems.at[GROUPS]),
        frames_copy(0, lead, GROUPS + 1),
    ]
    model_copies = [
        pltpu.make_async_copy(magnitude_hbm, magnitude_ref, sems.at[GROUPS + 2]),
        pltpu.make_async_copy(phase_hbm, phase_ref, sems.at[GROUPS + 3]),
    ]
    table_copy = pltpu.make_async_copy(table_hbm, table_ref, sems.at[GROUPS + 4])
    for copy in model_copies + copies:
        copy.start()
    for group in range(GROUPS):
        frames_copy(group * GROUP + lead, GROUP, group).start()
    table_copy.start()
    for copy in model_copies:
        copy.wait()
    magnitude, phase = magnitude_ref[...], phase_ref[...]
    model_ref[0:TILES, :] = magnitude * jnp.cos(phase)
    model_ref[TILES : 2 * TILES, :] = magnitude * jnp.sin(phase)
    model_ref[2 * TILES : 3 * TILES, :] = 1.0 / (magnitude * magnitude)
    for copy in copies:
        copy.wait()

    def group_step(group, carry):
        first = group * GROUP
        frames_copy(first + lead, GROUP, group).wait()
        for part in range(FOLD // 128):
            lanes = slice(part * 128, part * 128 + 128)
            sums = [jnp.zeros((OWNED, 128), F32)] * GROUP
            for fold in range(FOLDS):
                taps = [
                    jnp.broadcast_to(window_ref[fold, tap : tap + 1, lanes], (OWNED, 128))
                    for tap in range(TAPS)
                ]
                for frame in range(GROUP + TAPS - 1):
                    offset = (first + frame) * NFFT + fold * FOLD + part * 128
                    piece = volts_ref[:, pl.ds(pl.multiple_of(offset, 128), 128)]
                    piece = piece.astype(F32)
                    for tap in range(TAPS):
                        s = frame - tap
                        if 0 <= s < GROUP:
                            sums[s] = sums[s] + piece * taps[tap]
            for s in range(GROUP):
                row = pl.multiple_of((first + s) * OWNED, OWNED)
                folded_ref[part, pl.ds(row, OWNED), :] = sums[s]
        return carry

    lax.fori_loop(0, GROUPS, group_step, 0)
    pieces = []
    for part in range(FOLD // 128):
        pieces.append(
            jnp.concatenate(
                [folded_ref[part, pl.ds(j, SPECTRA, OWNED), :] for j in range(OWNED)],
                axis=0,
            )
        )
    folded = jnp.concatenate(pieces, axis=1)
    high = folded.astype(BF16)
    low = (folded - high.astype(F32)).astype(BF16)
    table_copy.wait()
    across = (((1,), (1,)), ((), ()))
    spectra = (
        lax.dot_general(table_ref[:, 0:FOLD], high, across, preferred_element_type=F32)
        + lax.dot_general(table_ref[:, 0:FOLD], low, across, preferred_element_type=F32)
        + lax.dot_general(
            table_ref[:, FOLD : 2 * FOLD], high, across, preferred_element_type=F32
        )
    )
    for part in range(2):
        for side in range(2):
            rows_ref[pl.ds(part * 2 + side, CHANNELS, 4), :] = spectra[
                part * CHANNELS : (part + 1) * CHANNELS, side * 128 : side * 128 + 128
            ]
    out_ref[...] = rows_ref[...].astype(BF16)


def channelize(volts, magnitude, phase):
    operands = (
        volts,
        jnp.asarray(fold_weights()),
        jnp.asarray(transform_weights()),
        magnitude.reshape(TILES, 128),
        phase.reshape(TILES, 128),
    )
    return pl.pallas_call(
        channelize_kernel,
        out_shape=[
            pltpu.VMEM((CHANNELS * 4, 128), BF16),
            pltpu.VMEM((3 * TILES, 128), F32),
        ],
        in_specs=[pl.BlockSpec(memory_space=pltpu.HBM)] * 5,
        scratch_shapes=[
            pltpu.VMEM(volts.shape, BF16),
            pltpu.VMEM((FOLDS, TAPS, FOLD), F32),
            pltpu.VMEM((2 * CHANNELS, 2 * FOLD), BF16),
            pltpu.VMEM((TILES, 128), F32),
            pltpu.VMEM((TILES, 128), F32),
            pltpu.VMEM((2, SPECTRA * OWNED, 128), F32),
            pltpu.VMEM((CHANNELS * 4, 128), F32),
            pltpu.SemaphoreType.DMA((GROUPS + 5,)),
        ],
        compiler_params=pltpu.CompilerParams(vmem_limit_bytes=8 * 2**20),
        name="channelize",
    )(*[pltpu.with_memory_space_constraint(x, pltpu.HBM) for x in operands])


def turn_spectra(source, wide_ref, real_ref, imag_ref):
    wide_ref[...] = source[...].astype(F32)
    unswap(wide_ref, 4)
    for part, target in ((0, real_ref), (1, imag_ref)):
        for group in range(2):
            block = wide_ref[pl.ds(part * 2 + group, 128, 4), :].T
            for j in range(4):
                target[group * 4 + j] = block[j * 32 : j * 32 + 32, :]


def build_lines(wide_ref, line_ref):
    lane = lax.broadcasted_iota(jnp.int32, (128, 128), 1)
    for group in range(2):
        real = wide_ref[pl.ds(group, 128, 4), :]
        imag = wide_ref[pl.ds(2 + group, 128, 4), :]
        for j in range(4):
            a = real if j == 0 else pltpu.roll(real, 128 - 32 * j, 1)
            b = imag if j == 1 else pltpu.roll(imag, (160 - 32 * j) % 128, 1)
            line_ref[pl.ds(group * 4 + j, 128, OWNED), :] = jnp.where(lane < 32, a, b)


def build_right(line_ref, right_ref):
    for block in range(HALF // 128):
        columns = slice(block * 128, block * 128 + 128)
        turned = line_ref[columns, :].T
        real, imag = turned[0:32].astype(BF16), turned[32:64].astype(BF16)
        right_ref[0, 0:32, columns] = real
        right_ref[0, 32:64, columns] = imag
        right_ref[1, 0:32, columns] = -imag
        right_ref[1, 32:64, columns] = real


def own_kernel(own_ref, real_ref, imag_ref, left_ref, right_ref, wide_ref, line_ref):
    turn_spectra(own_ref, wide_ref, real_ref, imag_ref)
    build_lines(wide_ref, line_ref)
    left_ref[...] = (line_ref[:, 0:64] * (1.0 / SPECTRA)).astype(BF16)
    build_right(line_ref, right_ref)


def own_turn(own):
    return pl.pallas_call(
        own_kernel,
        out_shape=[
            pltpu.VMEM((OWNED, SPECTRA, 128), F32),
            pltpu.VMEM((OWNED, SPECTRA, 128), F32),
            pltpu.VMEM((HALF, 2 * SPECTRA), BF16),
            pltpu.VMEM((2, 2 * SPECTRA, HALF), BF16),
        ],
        scratch_shapes=[pltpu.VMEM((512, 128), F32), pltpu.VMEM((HALF, 128), F32)],
        compiler_params=pltpu.CompilerParams(vmem_limit_bytes=8 * 2**20),
        cost_estimate=pl.CostEstimate(
            flops=2**22, bytes_accessed=2**20, transcendentals=0
        ),
        name="own_turn",
    )(own)


def solve_kernel(
    ownr_ref, owni_ref, other_ref, model_ref, out_ref,
    wide_ref, otherr_ref, otheri_ref, probe_ref, part_ref,
):
    turn_spectra(other_ref, wide_ref, otherr_ref, otheri_ref)
    tiles = 2 * OWNED

    def spectra_of(tile):
        if tile < OWNED:
            return ownr_ref[tile], owni_ref[tile]
        return otherr_ref[tile - OWNED], otheri_ref[tile - OWNED]

    def gathered(which):
        total = part_ref[which, pl.ds(0, tiles, 8), :]
        for row in range(1, 8):
            total = total + part_ref[which, pl.ds(row, tiles, 8), :]
        return total

    def eight(values):
        return (values[0:8] + values[8:16]) + (values[16:24] + values[24:32])

    for tile in range(tiles):
        real, imag = spectra_of(tile)
        part_ref[0, tile * 8 : tile * 8 + 8, :] = eight(real * real + imag * imag)
    diagonal = gathered(0) * (1.0 / SPECTRA)
    half = lax.axis_index("bl")

    def model(which):
        rows = [
            pl.ds(pl.multiple_of(which * tiles + side * OWNED, OWNED), OWNED)
            for side in (half, 1 - half)
        ]
        return jnp.concatenate([model_ref[r, :] for r in rows], axis=0)

    mreal, mimag, inverse = model(0), model(1), model(2)

    def single_step(greal, gimag):
        yreal = greal * mreal - gimag * mimag
        yimag = greal * mimag + gimag * mreal
        energy = jnp.sum(yreal * yreal + yimag * yimag, keepdims=True) + EPSILON
        factor = inverse / energy
        probe_ref[0] = yreal
        probe_ref[1] = yimag
        areal = jnp.zeros((SPECTRA, 128), F32)
        aimag = jnp.zeros((SPECTRA, 128), F32)
        for tile in range(tiles):
            real, imag = spectra_of(tile)
            pr = jnp.broadcast_to(probe_ref[0, tile : tile + 1, :], (SPECTRA, 128))
            pi = jnp.broadcast_to(probe_ref[1, tile : tile + 1, :], (SPECTRA, 128))
            areal = areal + (real * pr + imag * pi)
            aimag = aimag + (real * pi - imag * pr)
        sreal = jnp.broadcast_to(jnp.sum(areal, axis=1, keepdims=True), (SPECTRA, 128))
        simag = jnp.broadcast_to(jnp.sum(aimag, axis=1, keepdims=True), (SPECTRA, 128))
        for tile in range(tiles):
            real, imag = spectra_of(tile)
            rows = slice(tile * 8, tile * 8 + 8)
            part_ref[0, rows, :] = eight(real * sreal - imag * simag)
            part_ref[1, rows, :] = eight(real * simag + imag * sreal)
        wreal = gathered(0) * (1.0 / SPECTRA) - diagonal * yreal
        wimag = gathered(1) * (1.0 / SPECTRA) - diagonal * yimag
        return (
            (wreal * mreal + wimag * mimag) * factor,
            (wimag * mreal - wreal * mimag) * factor,
        )

    greal = jnp.ones((tiles, 128), F32)
    gimag = jnp.zeros((tiles, 128), F32)

    def double_step(_, gains):
        first = single_step(*gains)
        fresh = single_step(*first)
        return tuple((a + b) * 0.5 for a, b in zip(fresh, first))

    greal, gimag = lax.fori_loop(0, ITERS // 2, double_step, (greal, gimag))
    wide_ref[0:128, :] = jnp.zeros((128, 128), F32)
    wide_ref[0:8, :] = greal[0:OWNED, :]
    wide_ref[8:16, :] = gimag[0:OWNED, :]
    out_ref[...] = wide_ref[0:128, :].T
    unswap(out_ref, 1)


def solve(ownr, owni, other, model):
    tiles = 2 * OWNED
    return pl.pallas_call(
        solve_kernel,
        out_shape=pltpu.VMEM((128, 128), F32),
        scratch_shapes=[
            pltpu.VMEM((512, 128), F32),
            pltpu.VMEM((OWNED, SPECTRA, 128), F32),
            pltpu.VMEM((OWNED, SPECTRA, 128), F32),
            pltpu.VMEM((2, tiles, 128), F32),
            pltpu.VMEM((2, tiles * 8, 128), F32),
        ],
        compiler_params=pltpu.CompilerParams(vmem_limit_bytes=8 * 2**20),
        name="solve",
    )(ownr, owni, other, model)


WIDE = 1024
SLOTS = 4


def power_kernel(
    left_ref, mine_ref, other_ref, out_hbm, wide_ref, line_ref, right_ref, slots_ref, sems
):
    half = lax.axis_index("bl")
    pieces = HALF // WIDE

    def out_copy(count, part, start):
        slot = lax.rem(count, SLOTS)
        columns = pl.ds(pl.multiple_of(start, WIDE), WIDE)
        return pltpu.make_async_copy(
            slots_ref.at[slot], out_hbm.at[part, :, columns], sems.at[slot]
        )

    def products(right, side, done):
        def step(index, carry):
            part, piece = index // pieces, lax.rem(index, pieces)
            count = done + index
            first = pl.multiple_of(piece * WIDE, WIDE)
            copy = out_copy(count, part, side * HALF + first)

            @pl.when(count >= SLOTS)
            def _():
                copy.wait()

            slots_ref[lax.rem(count, SLOTS)] = jnp.dot(
                left_ref[...], right[part, :, pl.ds(first, WIDE)],
                preferred_element_type=F32,
            ).astype(BF16)
            copy.start()
            return carry

        lax.fori_loop(0, 2 * pieces, step, 0)

    products(mine_ref, half, 0)
    wide_ref[...] = other_ref[...].astype(F32)
    unswap(wide_ref, 4)
    build_lines(wide_ref, line_ref)
    build_right(line_ref, right_ref)
    products(right_ref, 1 - half, 2 * pieces)
    for slot in range(SLOTS):
        out_copy(slot, 0, 0).wait()


def power(left, mine, other):
    return pl.pallas_call(
        power_kernel,
        in_specs=[pl.BlockSpec(memory_space=pltpu.VMEM)] * 3,
        out_specs=pl.BlockSpec(memory_space=pltpu.HBM),
        out_shape=jax.ShapeDtypeStruct((2, HALF, 2 * HALF), BF16),
        scratch_shapes=[
            pltpu.VMEM((512, 128), F32),
            pltpu.VMEM((HALF, 128), F32),
            pltpu.VMEM((2, 2 * SPECTRA, HALF), BF16),
            pltpu.VMEM((SLOTS, HALF, WIDE), BF16),
            pltpu.SemaphoreType.DMA((SLOTS,)),
        ],
        compiler_params=pltpu.CompilerParams(vmem_limit_bytes=24 * 2**20),
        cost_estimate=pl.CostEstimate(
            flops=2 * 2 * 1024 * 2048 * 64, bytes_accessed=9 * 2**20, transcendentals=0
        ),
        name="power",
    )(left, mine, other)


def turn_kernel(gains_ref, out_ref, rows_ref):
    rows_ref[...] = gains_ref[...]
    unswap(rows_ref, 1)
    turned = rows_ref[...].T
    out_ref[0, 0] = turned[0:8, :]
    out_ref[1, 0] = turned[8:16, :]


def on_device(voltages, model_magnitude, model_phase):
    spectra, model = channelize(voltages[0], model_magnitude, model_phase)
    own = exchange(spectra.reshape(CHANNELS, 4, 128))
    own, model = lax.optimization_barrier((own, model))
    own = own.reshape(512, 128)
    other = lax.ppermute(own, "bl", [(0, 1), (1, 0)])
    model = model.reshape(6, 128, OWNED).transpose(0, 2, 1).reshape(3 * TILES, 128)
    ownr, owni, left, mine = own_turn(own)
    gains = solve(ownr, owni, other, model)
    moved = exchange(gains.reshape(128, 1, 128))
    visible = power(left, mine, other)
    gain_output = pl.pallas_call(
        turn_kernel,
        out_shape=jax.ShapeDtypeStruct((2, 1, OWNED, CHANNELS), F32),
        scratch_shapes=[pltpu.VMEM((128, 128), F32)],
        compiler_params=pltpu.CompilerParams(vmem_limit_bytes=2 * 2**20),
        name="turn",
    )(moved.reshape(128, 128))
    return visible[None], gain_output


def solution(mesh):
    in_specs = (P("bl", "gx", None), P("gx", None), P("gx", None))
    out_specs = (P("gx", None, "bl", None), P(None, "bl", "gx", None))
    return jax.shard_map(
        on_device, mesh=mesh, in_specs=in_specs, out_specs=out_specs, check_vma=False
    )
```

```python
import functools
import math

import jax
import jax.numpy as jnp
import numpy as np
from jax import lax
from jax.experimental import pallas as pl
from jax.experimental.pallas import tpu as pltpu
from jax.sharding import PartitionSpec as P

NFFT = 2048
TAPS = 4
SPECTRA = 32
ITERS = 4
CHANNELS = 128
OWNED = 8
HALF = 1024
EPSILON = 1e-06
F32 = jnp.float32
BF16 = jnp.bfloat16
FOLD = 256
FOLDS = NFFT // FOLD


SPECTRA_FIRST = 86
GAINS_FIRST = 54


def members(first):
    order = list(range(CHANNELS))
    order[0], order[first] = order[first], order[0]
    return order


def exchange(values, first):
    return lax.all_to_all(values, "gx", 0, 0, axis_index_groups=[members(first)])


def unswap(ref, rows, first):
    here, there = slice(0, rows), slice(first * rows, (first + 1) * rows)
    one, two = ref[here, :], ref[there, :]
    ref[here, :] = two
    ref[there, :] = one


def split_bf16(values):
    high = values.astype(np.float32).astype(jnp.bfloat16)
    low = (values - high.astype(np.float64)).astype(np.float32).astype(jnp.bfloat16)
    return high, low


def fold_weights():
    position = np.arange(TAPS * NFFT, dtype=np.float64) + 0.5
    hann = 0.5 - 0.5 * np.cos(2.0 * np.pi * position / (TAPS * NFFT))
    taper = np.sinc(position / NFFT - TAPS / 2.0) * hann
    taper = taper.reshape(TAPS, FOLDS, FOLD)
    signs = (-1.0) ** np.arange(FOLDS)
    folded = (taper * signs[None, :, None]).transpose(1, 0, 2)
    return folded.astype(np.float32)


def transform_weights():
    odd = 2 * np.array(members(SPECTRA_FIRST)) + 1
    phase = (odd[:, None] * np.arange(FOLD)[None, :]) % (2 * FOLD)
    angle = phase.astype(np.float64) * (2.0 * np.pi / (2 * FOLD))
    scale = 1.0 / math.sqrt(NFFT)
    table = np.concatenate([np.cos(angle), -np.sin(angle)], axis=0) * scale
    high, low = split_bf16(table)
    return np.concatenate([high, low], axis=1)


GROUP = 8
GROUPS = SPECTRA // GROUP
TILES = 2 * OWNED


def channelize_kernel(
    volts_hbm, window_hbm, table_hbm, magnitude_hbm, phase_hbm, out_ref, model_ref,
    volts_ref, window_ref, table_ref, folded_ref, rows_ref, sems,
):
    def frames_copy(first, count, slot):
        start = first * NFFT
        if not isinstance(first, int):
            start = pl.multiple_of(start, NFFT)
        span = pl.ds(start, count * NFFT)
        return pltpu.make_async_copy(
            volts_hbm.at[:, span], volts_ref.at[:, span], sems.at[slot]
        )

    lead = TAPS - 1
    copies = [
        pltpu.make_async_copy(window_hbm, window_ref, sems.at[GROUPS]),
        frames_copy(0, lead, GROUPS + 1),
    ]
    model_copies = [
        pltpu.make_async_copy(
            magnitude_hbm, model_ref.at[pl.ds(0, TILES), :], sems.at[GROUPS + 2]
        ),
        pltpu.make_async_copy(
            phase_hbm, model_ref.at[pl.ds(TILES, TILES), :], sems.at[GROUPS + 3]
        ),
    ]
    table_copy = pltpu.make_async_copy(table_hbm, table_ref, sems.at[GROUPS + 4])
    for copy in copies:
        copy.start()
    for group in range(GROUPS):
        frames_copy(group * GROUP + lead, GROUP, group).start()
    for copy in [table_copy] + model_copies:
        copy.start()
    for copy in copies:
        copy.wait()

    def group_step(group, carry):
        first = group * GROUP
        frames_copy(first + lead, GROUP, group).wait()
        for part in range(FOLD // 128):
            lanes = slice(part * 128, part * 128 + 128)
            sums = [jnp.zeros((OWNED, 128), F32)] * GROUP
            for fold in range(FOLDS):
                taps = [
                    jnp.broadcast_to(window_ref[fold, tap : tap + 1, lanes], (OWNED, 128))
                    for tap in range(TAPS)
                ]
                for frame in range(GROUP + TAPS - 1):
                    offset = (first + frame) * NFFT + fold * FOLD + part * 128
                    piece = volts_ref[:, pl.ds(pl.multiple_of(offset, 128), 128)]
                    piece = piece.astype(F32)
                    for tap in range(TAPS):
                        s = frame - tap
                        if 0 <= s < GROUP:
                            sums[s] = sums[s] + piece * taps[tap]
            for s in range(GROUP):
                row = pl.multiple_of((first + s) * OWNED, OWNED)
                folded_ref[part, pl.ds(row, OWNED), :] = sums[s]
        return carry

    lax.fori_loop(0, GROUPS, group_step, 0)
    pieces = []
    for part in range(FOLD // 128):
        pieces.append(
            jnp.concatenate(
                [folded_ref[part, pl.ds(j, SPECTRA, OWNED), :] for j in range(OWNED)],
                axis=0,
            )
        )
    folded = jnp.concatenate(pieces, axis=1)
    high = folded.astype(BF16)
    low = (folded - high.astype(F32)).astype(BF16)
    table_copy.wait()
    across = (((1,), (1,)), ((), ()))
    spectra = (
        lax.dot_general(table_ref[:, 0:FOLD], high, across, preferred_element_type=F32)
        + lax.dot_general(table_ref[:, 0:FOLD], low, across, preferred_element_type=F32)
        + lax.dot_general(
            table_ref[:, FOLD : 2 * FOLD], high, across, preferred_element_type=F32
        )
    )
    for part in range(2):
        for side in range(2):
            rows_ref[pl.ds(part * 2 + side, CHANNELS, 4), :] = spectra[
                part * CHANNELS : (part + 1) * CHANNELS, side * 128 : side * 128 + 128
            ]
    out_ref[...] = rows_ref[...].astype(BF16)
    for copy in model_copies:
        copy.wait()


def channelize(volts, magnitude, phase):
    operands = (
        volts,
        jnp.asarray(fold_weights()),
        jnp.asarray(transform_weights()),
        magnitude.reshape(TILES, 128),
        phase.reshape(TILES, 128),
    )
    return pl.pallas_call(
        channelize_kernel,
        out_shape=[
            pltpu.VMEM((CHANNELS * 4, 128), BF16),
            pltpu.VMEM((2 * TILES, 128), F32),
        ],
        in_specs=[pl.BlockSpec(memory_space=pltpu.HBM)] * 5,
        scratch_shapes=[
            pltpu.VMEM(volts.shape, BF16),
            pltpu.VMEM((FOLDS, TAPS, FOLD), F32),
            pltpu.VMEM((2 * CHANNELS, 2 * FOLD), BF16),
            pltpu.VMEM((2, SPECTRA * OWNED, 128), F32),
            pltpu.VMEM((CHANNELS * 4, 128), F32),
            pltpu.SemaphoreType.DMA((GROUPS + 5,)),
        ],
        compiler_params=pltpu.CompilerParams(vmem_limit_bytes=8 * 2**20),
        name="channelize",
    )(*[pltpu.with_memory_space_constraint(x, pltpu.HBM) for x in operands])


def turn_spectra(source, wide_ref, real_ref, imag_ref):
    wide_ref[...] = source[...].astype(F32)
    unswap(wide_ref, 4, SPECTRA_FIRST)
    for part, target in ((0, real_ref), (1, imag_ref)):
        for group in range(2):
            block = wide_ref[pl.ds(part * 2 + group, 128, 4), :].T
            for j in range(4):
                target[group * 4 + j] = block[j * 32 : j * 32 + 32, :]


def build_lines(wide_ref, line_ref):
    lane = lax.broadcasted_iota(jnp.int32, (128, 128), 1)
    for group in range(2):
        real = wide_ref[pl.ds(group, 128, 4), :]
        imag = wide_ref[pl.ds(2 + group, 128, 4), :]
        for j in range(4):
            a = real if j == 0 else pltpu.roll(real, 128 - 32 * j, 1)
            b = imag if j == 1 else pltpu.roll(imag, (160 - 32 * j) % 128, 1)
            line_ref[pl.ds(group * 4 + j, 128, OWNED), :] = jnp.where(lane < 32, a, b)


def build_right(line_ref, right_ref):
    for block in range(HALF // 128):
        columns = slice(block * 128, block * 128 + 128)
        turned = line_ref[columns, :].T
        real, imag = turned[0:32].astype(BF16), turned[32:64].astype(BF16)
        right_ref[0, 0:32, columns] = real
        right_ref[0, 32:64, columns] = imag
        right_ref[1, 0:32, columns] = -imag
        right_ref[1, 32:64, columns] = real


def own_kernel(
    own_ref, raw_ref, real_ref, imag_ref, left_ref, right_ref, model_ref,
    wide_ref, line_ref,
):
    magnitude, phase = raw_ref[0:TILES, :], raw_ref[TILES : 2 * TILES, :]
    model_ref[0:TILES, :] = magnitude * jnp.cos(phase)
    model_ref[TILES : 2 * TILES, :] = magnitude * jnp.sin(phase)
    model_ref[2 * TILES : 3 * TILES, :] = 1.0 / (magnitude * magnitude)
    turn_spectra(own_ref, wide_ref, real_ref, imag_ref)
    build_lines(wide_ref, line_ref)
    left_ref[...] = (line_ref[:, 0:64] * (1.0 / SPECTRA)).astype(BF16)
    build_right(line_ref, right_ref)


def own_turn(own, raw):
    return pl.pallas_call(
        own_kernel,
        out_shape=[
            pltpu.VMEM((OWNED, SPECTRA, 128), F32),
            pltpu.VMEM((OWNED, SPECTRA, 128), F32),
            pltpu.VMEM((HALF, 2 * SPECTRA), BF16),
            pltpu.VMEM((2, 2 * SPECTRA, HALF), BF16),
            pltpu.VMEM((3 * TILES, 128), F32),
        ],
        scratch_shapes=[pltpu.VMEM((512, 128), F32), pltpu.VMEM((HALF, 128), F32)],
        compiler_params=pltpu.CompilerParams(vmem_limit_bytes=8 * 2**20),
        cost_estimate=pl.CostEstimate(
            flops=2**22, bytes_accessed=2**20, transcendentals=0
        ),
        name="own_turn",
    )(own, raw)


def solve_kernel(
    ownr_ref, owni_ref, other_ref, model_ref, out_ref,
    wide_ref, otherr_ref, otheri_ref, probe_ref, part_ref,
):
    turn_spectra(other_ref, wide_ref, otherr_ref, otheri_ref)
    tiles = 2 * OWNED

    def spectra_of(tile):
        if tile < OWNED:
            return ownr_ref[tile], owni_ref[tile]
        return otherr_ref[tile - OWNED], otheri_ref[tile - OWNED]

    def gathered(which):
        total = part_ref[which, pl.ds(0, tiles, 8), :]
        for row in range(1, 8):
            total = total + part_ref[which, pl.ds(row, tiles, 8), :]
        return total

    def eight(values):
        return (values[0:8] + values[8:16]) + (values[16:24] + values[24:32])

    for tile in range(tiles):
        real, imag = spectra_of(tile)
        part_ref[0, tile * 8 : tile * 8 + 8, :] = eight(real * real + imag * imag)
    diagonal = gathered(0) * (1.0 / SPECTRA)
    half = lax.axis_index("bl")

    def model(which):
        rows = [
            pl.ds(pl.multiple_of(which * tiles + side * OWNED, OWNED), OWNED)
            for side in (half, 1 - half)
        ]
        return jnp.concatenate([model_ref[r, :] for r in rows], axis=0)

    mreal, mimag, inverse = model(0), model(1), model(2)

    def single_step(greal, gimag):
        yreal = greal * mreal - gimag * mimag
        yimag = greal * mimag + gimag * mreal
        energy = jnp.sum(yreal * yreal + yimag * yimag, keepdims=True) + EPSILON
        factor = inverse / energy
        probe_ref[0] = yreal
        probe_ref[1] = yimag
        areal = jnp.zeros((SPECTRA, 128), F32)
        aimag = jnp.zeros((SPECTRA, 128), F32)
        for tile in range(tiles):
            real, imag = spectra_of(tile)
            pr = jnp.broadcast_to(probe_ref[0, tile : tile + 1, :], (SPECTRA, 128))
            pi = jnp.broadcast_to(probe_ref[1, tile : tile + 1, :], (SPECTRA, 128))
            areal = areal + (real * pr + imag * pi)
            aimag = aimag + (real * pi - imag * pr)
        sreal = jnp.broadcast_to(jnp.sum(areal, axis=1, keepdims=True), (SPECTRA, 128))
        simag = jnp.broadcast_to(jnp.sum(aimag, axis=1, keepdims=True), (SPECTRA, 128))
        for tile in range(tiles):
            real, imag = spectra_of(tile)
            rows = slice(tile * 8, tile * 8 + 8)
            part_ref[0, rows, :] = eight(real * sreal - imag * simag)
            part_ref[1, rows, :] = eight(real * simag + imag * sreal)
        wreal = gathered(0) * (1.0 / SPECTRA) - diagonal * yreal
        wimag = gathered(1) * (1.0 / SPECTRA) - diagonal * yimag
        return (
            (wreal * mreal + wimag * mimag) * factor,
            (wimag * mreal - wreal * mimag) * factor,
        )

    greal = jnp.ones((tiles, 128), F32)
    gimag = jnp.zeros((tiles, 128), F32)

    def double_step(_, gains):
        first = single_step(*gains)
        fresh = single_step(*first)
        return tuple((a + b) * 0.5 for a, b in zip(fresh, first))

    greal, gimag = lax.fori_loop(0, ITERS // 2, double_step, (greal, gimag))
    wide_ref[0:128, :] = jnp.zeros((128, 128), F32)
    wide_ref[0:8, :] = greal[0:OWNED, :]
    wide_ref[8:16, :] = gimag[0:OWNED, :]
    out_ref[...] = wide_ref[0:128, :].T
    unswap(out_ref, 1, GAINS_FIRST)


def solve(ownr, owni, other, model):
    tiles = 2 * OWNED
    return pl.pallas_call(
        solve_kernel,
        out_shape=pltpu.VMEM((128, 128), F32),
        scratch_shapes=[
            pltpu.VMEM((512, 128), F32),
            pltpu.VMEM((OWNED, SPECTRA, 128), F32),
            pltpu.VMEM((OWNED, SPECTRA, 128), F32),
            pltpu.VMEM((2, tiles, 128), F32),
            pltpu.VMEM((2, tiles * 8, 128), F32),
        ],
        compiler_params=pltpu.CompilerParams(vmem_limit_bytes=8 * 2**20),
        name="solve",
    )(ownr, owni, other, model)


WIDE = 1024
SLOTS = 4


def power_kernel(
    left_ref, mine_ref, other_ref, out_hbm, wide_ref, line_ref, right_ref, slots_ref, sems
):
    half = lax.axis_index("bl")
    pieces = HALF // WIDE

    def out_copy(count, part, start):
        slot = lax.rem(count, SLOTS)
        columns = pl.ds(pl.multiple_of(start, WIDE), WIDE)
        return pltpu.make_async_copy(
            slots_ref.at[slot], out_hbm.at[part, :, columns], sems.at[slot]
        )

    def products(right, side, done):
        def step(index, carry):
            part, piece = index // pieces, lax.rem(index, pieces)
            count = done + index
            first = pl.multiple_of(piece * WIDE, WIDE)
            copy = out_copy(count, part, side * HALF + first)

            @pl.when(count >= SLOTS)
            def _():
                copy.wait()

            slots_ref[lax.rem(count, SLOTS)] = jnp.dot(
                left_ref[...], right[part, :, pl.ds(first, WIDE)],
                preferred_element_type=F32,
            ).astype(BF16)
            copy.start()
            return carry

        lax.fori_loop(0, 2 * pieces, step, 0)

    products(mine_ref, half, 0)
    wide_ref[...] = other_ref[...].astype(F32)
    unswap(wide_ref, 4, SPECTRA_FIRST)
    build_lines(wide_ref, line_ref)
    build_right(line_ref, right_ref)
    products(right_ref, 1 - half, 2 * pieces)
    for slot in range(SLOTS):
        out_copy(slot, 0, 0).wait()


def power(left, mine, other):
    return pl.pallas_call(
        power_kernel,
        in_specs=[pl.BlockSpec(memory_space=pltpu.VMEM)] * 3,
        out_specs=pl.BlockSpec(memory_space=pltpu.HBM),
        out_shape=jax.ShapeDtypeStruct((2, HALF, 2 * HALF), BF16),
        scratch_shapes=[
            pltpu.VMEM((512, 128), F32),
            pltpu.VMEM((HALF, 128), F32),
            pltpu.VMEM((2, 2 * SPECTRA, HALF), BF16),
            pltpu.VMEM((SLOTS, HALF, WIDE), BF16),
            pltpu.SemaphoreType.DMA((SLOTS,)),
        ],
        compiler_params=pltpu.CompilerParams(vmem_limit_bytes=24 * 2**20),
        cost_estimate=pl.CostEstimate(
            flops=2 * 2 * 1024 * 2048 * 64, bytes_accessed=9 * 2**20, transcendentals=0
        ),
        name="power",
    )(left, mine, other)


def turn_kernel(gains_ref, out_ref, rows_ref):
    rows_ref[...] = gains_ref[...]
    unswap(rows_ref, 1, GAINS_FIRST)
    turned = rows_ref[...].T
    out_ref[0, 0] = turned[0:8, :]
    out_ref[1, 0] = turned[8:16, :]


def on_device(voltages, model_magnitude, model_phase):
    spectra, raw = channelize(voltages[0], model_magnitude, model_phase)
    own = exchange(spectra.reshape(CHANNELS, 4, 128), SPECTRA_FIRST)
    own = own.reshape(512, 128)
    other = lax.ppermute(own, "bl", [(0, 1), (1, 0)])
    ownr, owni, left, mine, model = own_turn(own, raw)
    model = model.reshape(6, 128, OWNED).transpose(0, 2, 1).reshape(3 * TILES, 128)
    gains = solve(ownr, owni, other, model)
    moved = exchange(gains.reshape(128, 1, 128), GAINS_FIRST)
    visible = power(left, mine, other)
    gain_output = pl.pallas_call(
        turn_kernel,
        out_shape=jax.ShapeDtypeStruct((2, 1, OWNED, CHANNELS), F32),
        scratch_shapes=[pltpu.VMEM((128, 128), F32)],
        compiler_params=pltpu.CompilerParams(vmem_limit_bytes=2 * 2**20),
        name="turn",
    )(moved.reshape(128, 128))
    return visible[None], gain_output


def solution(mesh):
    in_specs = (P("bl", "gx", None), P("gx", None), P("gx", None))
    out_specs = (P("gx", None, "bl", None), P(None, "bl", "gx", None))
    return jax.shard_map(
        on_device, mesh=mesh, in_specs=in_specs, out_specs=out_specs, check_vma=False
    )
```

```python
import functools
import math

import jax
import jax.numpy as jnp
import numpy as np
from jax import lax
from jax.experimental import pallas as pl
from jax.experimental.pallas import tpu as pltpu
from jax.sharding import PartitionSpec as P

NFFT = 2048
TAPS = 4
SPECTRA = 32
ITERS = 4
CHANNELS = 128
OWNED = 8
HALF = 1024
EPSILON = 1e-06
F32 = jnp.float32
BF16 = jnp.bfloat16
FOLD = 256
FOLDS = NFFT // FOLD


SPECTRA_FIRST = 90
GAINS_FIRST = 54


def members(first):
    order = list(range(CHANNELS))
    order[0], order[first] = order[first], order[0]
    return order


def exchange(values, first):
    return lax.all_to_all(values, "gx", 0, 0, axis_index_groups=[members(first)])


def unswap(ref, rows, first):
    here, there = slice(0, rows), slice(first * rows, (first + 1) * rows)
    one, two = ref[here, :], ref[there, :]
    ref[here, :] = two
    ref[there, :] = one


def split_bf16(values):
    high = values.astype(np.float32).astype(jnp.bfloat16)
    low = (values - high.astype(np.float64)).astype(np.float32).astype(jnp.bfloat16)
    return high, low


def fold_weights():
    position = np.arange(TAPS * NFFT, dtype=np.float64) + 0.5
    hann = 0.5 - 0.5 * np.cos(2.0 * np.pi * position / (TAPS * NFFT))
    taper = np.sinc(position / NFFT - TAPS / 2.0) * hann
    taper = taper.reshape(TAPS, FOLDS, FOLD)
    signs = (-1.0) ** np.arange(FOLDS)
    folded = (taper * signs[None, :, None]).transpose(1, 0, 2)
    return folded.astype(np.float32)


def transform_weights():
    odd = 2 * np.array(members(SPECTRA_FIRST)) + 1
    phase = (odd[:, None] * np.arange(FOLD)[None, :]) % (2 * FOLD)
    angle = phase.astype(np.float64) * (2.0 * np.pi / (2 * FOLD))
    scale = 1.0 / math.sqrt(NFFT)
    table = np.concatenate([np.cos(angle), -np.sin(angle)], axis=0) * scale
    high, low = split_bf16(table)
    return np.concatenate([high, low], axis=1)


GROUP = 8
GROUPS = SPECTRA // GROUP
TILES = 2 * OWNED


def channelize_kernel(
    volts_hbm, window_hbm, table_hbm, magnitude_hbm, phase_hbm, out_ref, model_ref,
    volts_ref, window_ref, table_ref, folded_ref, rows_ref, sems,
):
    def frames_copy(first, count, slot):
        span = pl.ds(first * NFFT, count * NFFT)
        return pltpu.make_async_copy(
            volts_hbm.at[:, span], volts_ref.at[:, span], sems.at[slot]
        )

    lead = TAPS - 1
    copies = [
        pltpu.make_async_copy(window_hbm, window_ref, sems.at[GROUPS]),
        frames_copy(0, lead, GROUPS + 1),
    ]
    model_copies = [
        pltpu.make_async_copy(
            magnitude_hbm, model_ref.at[pl.ds(0, TILES), :], sems.at[GROUPS + 2]
        ),
        pltpu.make_async_copy(
            phase_hbm, model_ref.at[pl.ds(TILES, TILES), :], sems.at[GROUPS + 3]
        ),
    ]
    table_copy = pltpu.make_async_copy(table_hbm, table_ref, sems.at[GROUPS + 4])
    for copy in copies:
        copy.start()
    for group in range(GROUPS):
        frames_copy(group * GROUP + lead, GROUP, group).start()
    for copy in [table_copy] + model_copies:
        copy.start()
    for copy in copies:
        copy.wait()

    def group_step(group):
        first = group * GROUP
        frames_copy(first + lead, GROUP, group).wait()
        for part in range(FOLD // 128):
            lanes = slice(part * 128, part * 128 + 128)
            sums = [jnp.zeros((OWNED, 128), F32)] * GROUP
            for fold in range(FOLDS):
                taps = [
                    jnp.broadcast_to(window_ref[fold, tap : tap + 1, lanes], (OWNED, 128))
                    for tap in range(TAPS)
                ]
                for frame in range(GROUP + TAPS - 1):
                    offset = (first + frame) * NFFT + fold * FOLD + part * 128
                    piece = volts_ref[:, pl.ds(offset, 128)]
                    piece = piece.astype(F32)
                    for tap in range(TAPS):
                        s = frame - tap
                        if 0 <= s < GROUP:
                            sums[s] = sums[s] + piece * taps[tap]
            for s in range(GROUP):
                row = (first + s) * OWNED
                folded_ref[part, pl.ds(row, OWNED), :] = sums[s]

    for group in range(GROUPS):
        group_step(group)
    pieces = []
    for part in range(FOLD // 128):
        pieces.append(
            jnp.concatenate(
                [folded_ref[part, pl.ds(j, SPECTRA, OWNED), :] for j in range(OWNED)],
                axis=0,
            )
        )
    folded = jnp.concatenate(pieces, axis=1)
    high = folded.astype(BF16)
    low = (folded - high.astype(F32)).astype(BF16)
    table_copy.wait()
    across = (((1,), (1,)), ((), ()))
    spectra = (
        lax.dot_general(table_ref[:, 0:FOLD], high, across, preferred_element_type=F32)
        + lax.dot_general(table_ref[:, 0:FOLD], low, across, preferred_element_type=F32)
        + lax.dot_general(
            table_ref[:, FOLD : 2 * FOLD], high, across, preferred_element_type=F32
        )
    )
    for part in range(2):
        for side in range(2):
            rows_ref[pl.ds(part * 2 + side, CHANNELS, 4), :] = spectra[
                part * CHANNELS : (part + 1) * CHANNELS, side * 128 : side * 128 + 128
            ]
    out_ref[...] = rows_ref[...].astype(BF16)
    for copy in model_copies:
        copy.wait()


def channelize(volts, magnitude, phase):
    operands = (
        volts,
        jnp.asarray(fold_weights()),
        jnp.asarray(transform_weights()),
        magnitude.reshape(TILES, 128),
        phase.reshape(TILES, 128),
    )
    return pl.pallas_call(
        channelize_kernel,
        out_shape=[
            pltpu.VMEM((CHANNELS * 4, 128), BF16),
            pltpu.VMEM((2 * TILES, 128), F32),
        ],
        in_specs=[pl.BlockSpec(memory_space=pltpu.HBM)] * 5,
        scratch_shapes=[
            pltpu.VMEM(volts.shape, BF16),
            pltpu.VMEM((FOLDS, TAPS, FOLD), F32),
            pltpu.VMEM((2 * CHANNELS, 2 * FOLD), BF16),
            pltpu.VMEM((2, SPECTRA * OWNED, 128), F32),
            pltpu.VMEM((CHANNELS * 4, 128), F32),
            pltpu.SemaphoreType.DMA((GROUPS + 5,)),
        ],
        compiler_params=pltpu.CompilerParams(vmem_limit_bytes=8 * 2**20),
        name="channelize",
    )(*[pltpu.with_memory_space_constraint(x, pltpu.HBM) for x in operands])


def turn_spectra(source, wide_ref, real_ref, imag_ref):
    wide_ref[...] = source[...].astype(F32)
    unswap(wide_ref, 4, SPECTRA_FIRST)
    for part, target in ((0, real_ref), (1, imag_ref)):
        for group in range(2):
            block = wide_ref[pl.ds(part * 2 + group, 128, 4), :].T
            for j in range(4):
                target[group * 4 + j] = block[j * 32 : j * 32 + 32, :]


def build_lines(wide_ref, line_ref):
    lane = lax.broadcasted_iota(jnp.int32, (128, 128), 1)
    for group in range(2):
        real = wide_ref[pl.ds(group, 128, 4), :]
        imag = wide_ref[pl.ds(2 + group, 128, 4), :]
        for j in range(4):
            a = real if j == 0 else pltpu.roll(real, 128 - 32 * j, 1)
            b = imag if j == 1 else pltpu.roll(imag, (160 - 32 * j) % 128, 1)
            line_ref[pl.ds(group * 4 + j, 128, OWNED), :] = jnp.where(lane < 32, a, b)


def build_right(line_ref, right_ref):
    for block in range(HALF // 128):
        columns = slice(block * 128, block * 128 + 128)
        turned = line_ref[columns, :].T
        real, imag = turned[0:32].astype(BF16), turned[32:64].astype(BF16)
        right_ref[0, 0:32, columns] = real
        right_ref[0, 32:64, columns] = imag
        right_ref[1, 0:32, columns] = -imag
        right_ref[1, 32:64, columns] = real


def own_kernel(
    own_ref, raw_ref, real_ref, imag_ref, left_ref, right_ref, model_ref,
    wide_ref, line_ref,
):
    magnitude, phase = raw_ref[0:TILES, :], raw_ref[TILES : 2 * TILES, :]
    model_ref[0:TILES, :] = magnitude * jnp.cos(phase)
    model_ref[TILES : 2 * TILES, :] = magnitude * jnp.sin(phase)
    model_ref[2 * TILES : 3 * TILES, :] = 1.0 / (magnitude * magnitude)
    turn_spectra(own_ref, wide_ref, real_ref, imag_ref)
    build_lines(wide_ref, line_ref)
    left_ref[...] = (line_ref[:, 0:64] * (1.0 / SPECTRA)).astype(BF16)
    build_right(line_ref, right_ref)


def own_turn(own, raw):
    return pl.pallas_call(
        own_kernel,
        out_shape=[
            pltpu.VMEM((OWNED, SPECTRA, 128), F32),
            pltpu.VMEM((OWNED, SPECTRA, 128), F32),
            pltpu.VMEM((HALF, 2 * SPECTRA), BF16),
            pltpu.VMEM((2, 2 * SPECTRA, HALF), BF16),
            pltpu.VMEM((3 * TILES, 128), F32),
        ],
        scratch_shapes=[pltpu.VMEM((512, 128), F32), pltpu.VMEM((HALF, 128), F32)],
        compiler_params=pltpu.CompilerParams(vmem_limit_bytes=8 * 2**20),
        cost_estimate=pl.CostEstimate(
            flops=2**22, bytes_accessed=2**20, transcendentals=0
        ),
        name="own_turn",
    )(own, raw)


def solve_kernel(
    ownr_ref, owni_ref, other_ref, model_ref, out_ref,
    wide_ref, otherr_ref, otheri_ref, probe_ref, part_ref,
):
    turn_spectra(other_ref, wide_ref, otherr_ref, otheri_ref)
    tiles = 2 * OWNED

    def spectra_of(tile):
        if tile < OWNED:
            return ownr_ref[tile], owni_ref[tile]
        return otherr_ref[tile - OWNED], otheri_ref[tile - OWNED]

    def gathered(which):
        total = part_ref[which, pl.ds(0, tiles, 8), :]
        for row in range(1, 8):
            total = total + part_ref[which, pl.ds(row, tiles, 8), :]
        return total

    def eight(values):
        return (values[0:8] + values[8:16]) + (values[16:24] + values[24:32])

    for tile in range(tiles):
        real, imag = spectra_of(tile)
        part_ref[0, tile * 8 : tile * 8 + 8, :] = eight(real * real + imag * imag)
    diagonal = gathered(0) * (1.0 / SPECTRA)
    half = lax.axis_index("bl")

    def model(which):
        rows = [
            pl.ds(pl.multiple_of(which * tiles + side * OWNED, OWNED), OWNED)
            for side in (half, 1 - half)
        ]
        return jnp.concatenate([model_ref[r, :] for r in rows], axis=0)

    mreal, mimag, inverse = model(0), model(1), model(2)

    def single_step(greal, gimag):
        yreal = greal * mreal - gimag * mimag
        yimag = greal * mimag + gimag * mreal
        energy = jnp.sum(yreal * yreal + yimag * yimag, keepdims=True) + EPSILON
        factor = inverse / energy
        probe_ref[0] = yreal
        probe_ref[1] = yimag
        areal = jnp.zeros((SPECTRA, 128), F32)
        aimag = jnp.zeros((SPECTRA, 128), F32)
        for tile in range(tiles):
            real, imag = spectra_of(tile)
            pr = jnp.broadcast_to(probe_ref[0, tile : tile + 1, :], (SPECTRA, 128))
            pi = jnp.broadcast_to(probe_ref[1, tile : tile + 1, :], (SPECTRA, 128))
            areal = areal + (real * pr + imag * pi)
            aimag = aimag + (real * pi - imag * pr)
        sreal = jnp.broadcast_to(jnp.sum(areal, axis=1, keepdims=True), (SPECTRA, 128))
        simag = jnp.broadcast_to(jnp.sum(aimag, axis=1, keepdims=True), (SPECTRA, 128))
        for tile in range(tiles):
            real, imag = spectra_of(tile)
            rows = slice(tile * 8, tile * 8 + 8)
            part_ref[0, rows, :] = eight(real * sreal - imag * simag)
            part_ref[1, rows, :] = eight(real * simag + imag * sreal)
        wreal = gathered(0) * (1.0 / SPECTRA) - diagonal * yreal
        wimag = gathered(1) * (1.0 / SPECTRA) - diagonal * yimag
        return (
            (wreal * mreal + wimag * mimag) * factor,
            (wimag * mreal - wreal * mimag) * factor,
        )

    greal = jnp.ones((tiles, 128), F32)
    gimag = jnp.zeros((tiles, 128), F32)

    def double_step(_, gains):
        first = single_step(*gains)
        fresh = single_step(*first)
        return tuple((a + b) * 0.5 for a, b in zip(fresh, first))

    greal, gimag = lax.fori_loop(0, ITERS // 2, double_step, (greal, gimag))
    wide_ref[0:128, :] = jnp.zeros((128, 128), F32)
    wide_ref[0:8, :] = greal[0:OWNED, :]
    wide_ref[8:16, :] = gimag[0:OWNED, :]
    out_ref[...] = wide_ref[0:128, :].T
    unswap(out_ref, 1, GAINS_FIRST)


def solve(ownr, owni, other, model):
    tiles = 2 * OWNED
    return pl.pallas_call(
        solve_kernel,
        out_shape=pltpu.VMEM((128, 128), F32),
        scratch_shapes=[
            pltpu.VMEM((512, 128), F32),
            pltpu.VMEM((OWNED, SPECTRA, 128), F32),
            pltpu.VMEM((OWNED, SPECTRA, 128), F32),
            pltpu.VMEM((2, tiles, 128), F32),
            pltpu.VMEM((2, tiles * 8, 128), F32),
        ],
        compiler_params=pltpu.CompilerParams(vmem_limit_bytes=8 * 2**20),
        name="solve",
    )(ownr, owni, other, model)


WIDE = 1024
SLOTS = 4


def power_kernel(
    left_ref, mine_ref, other_ref, out_hbm, wide_ref, line_ref, right_ref, slots_ref, sems
):
    half = lax.axis_index("bl")
    pieces = HALF // WIDE

    def out_copy(count, part, start):
        slot = lax.rem(count, SLOTS)
        columns = pl.ds(pl.multiple_of(start, WIDE), WIDE)
        return pltpu.make_async_copy(
            slots_ref.at[slot], out_hbm.at[part, :, columns], sems.at[slot]
        )

    def products(right, side, done):
        def step(index, carry):
            part, piece = index // pieces, lax.rem(index, pieces)
            count = done + index
            first = pl.multiple_of(piece * WIDE, WIDE)
            copy = out_copy(count, part, side * HALF + first)

            @pl.when(count >= SLOTS)
            def _():
                copy.wait()

            slots_ref[lax.rem(count, SLOTS)] = jnp.dot(
                left_ref[...], right[part, :, pl.ds(first, WIDE)],
                preferred_element_type=F32,
            ).astype(BF16)
            copy.start()
            return carry

        lax.fori_loop(0, 2 * pieces, step, 0)

    products(mine_ref, half, 0)
    wide_ref[...] = other_ref[...].astype(F32)
    unswap(wide_ref, 4, SPECTRA_FIRST)
    build_lines(wide_ref, line_ref)
    build_right(line_ref, right_ref)
    products(right_ref, 1 - half, 2 * pieces)
    for slot in range(SLOTS):
        out_copy(slot, 0, 0).wait()


def power(left, mine, other):
    return pl.pallas_call(
        power_kernel,
        in_specs=[pl.BlockSpec(memory_space=pltpu.VMEM)] * 3,
        out_specs=pl.BlockSpec(memory_space=pltpu.HBM),
        out_shape=jax.ShapeDtypeStruct((2, HALF, 2 * HALF), BF16),
        scratch_shapes=[
            pltpu.VMEM((512, 128), F32),
            pltpu.VMEM((HALF, 128), F32),
            pltpu.VMEM((2, 2 * SPECTRA, HALF), BF16),
            pltpu.VMEM((SLOTS, HALF, WIDE), BF16),
            pltpu.SemaphoreType.DMA((SLOTS,)),
        ],
        compiler_params=pltpu.CompilerParams(vmem_limit_bytes=24 * 2**20),
        cost_estimate=pl.CostEstimate(
            flops=2 * 2 * 1024 * 2048 * 64, bytes_accessed=9 * 2**20, transcendentals=0
        ),
        name="power",
    )(left, mine, other)


def turn_kernel(gains_ref, out_ref, rows_ref):
    rows_ref[...] = gains_ref[...]
    unswap(rows_ref, 1, GAINS_FIRST)
    turned = rows_ref[...].T
    out_ref[0, 0] = turned[0:8, :]
    out_ref[1, 0] = turned[8:16, :]


def on_device(voltages, model_magnitude, model_phase):
    spectra, raw = channelize(voltages[0], model_magnitude, model_phase)
    own = exchange(spectra.reshape(CHANNELS, 4, 128), SPECTRA_FIRST)
    own = own.reshape(512, 128)
    other = lax.ppermute(own, "bl", [(0, 1), (1, 0)])
    ownr, owni, left, mine, model = own_turn(own, raw)
    model = model.reshape(6, 128, OWNED).transpose(0, 2, 1).reshape(3 * TILES, 128)
    gains = solve(ownr, owni, other, model)
    moved = exchange(gains.reshape(128, 1, 128), GAINS_FIRST)
    visible = power(left, mine, other)
    gain_output = pl.pallas_call(
        turn_kernel,
        out_shape=jax.ShapeDtypeStruct((2, 1, OWNED, CHANNELS), F32),
        scratch_shapes=[pltpu.VMEM((128, 128), F32)],
        compiler_params=pltpu.CompilerParams(vmem_limit_bytes=2 * 2**20),
        name="turn",
    )(moved.reshape(128, 128))
    return visible[None], gain_output


def solution(mesh):
    in_specs = (P("bl", "gx", None), P("gx", None), P("gx", None))
    out_specs = (P("gx", None, "bl", None), P(None, "bl", "gx", None))
    return jax.shard_map(
        on_device, mesh=mesh, in_specs=in_specs, out_specs=out_specs, check_vma=False
    )
```

```python
import functools
import math

import jax
import jax.numpy as jnp
import numpy as np
from jax import lax
from jax.experimental import pallas as pl
from jax.experimental.pallas import tpu as pltpu
from jax.sharding import PartitionSpec as P

NFFT = 2048
TAPS = 4
SPECTRA = 32
ITERS = 4
CHANNELS = 128
OWNED = 8
HALF = 1024
EPSILON = 1e-06
F32 = jnp.float32
BF16 = jnp.bfloat16
FOLD = 256
FOLDS = NFFT // FOLD


SPECTRA_FIRST = 90
GAINS_FIRST = 54


def members(first):
    order = list(range(CHANNELS))
    order[0], order[first] = order[first], order[0]
    return order


def exchange(values, first):
    return lax.all_to_all(values, "gx", 0, 0, axis_index_groups=[members(first)])


def unswap(ref, rows, first):
    here, there = slice(0, rows), slice(first * rows, (first + 1) * rows)
    one, two = ref[here, :], ref[there, :]
    ref[here, :] = two
    ref[there, :] = one


def split_bf16(values):
    high = values.astype(np.float32).astype(jnp.bfloat16)
    low = (values - high.astype(np.float64)).astype(np.float32).astype(jnp.bfloat16)
    return high, low


def fold_weights():
    position = np.arange(TAPS * NFFT, dtype=np.float64) + 0.5
    hann = 0.5 - 0.5 * np.cos(2.0 * np.pi * position / (TAPS * NFFT))
    taper = np.sinc(position / NFFT - TAPS / 2.0) * hann
    taper = taper.reshape(TAPS, FOLDS, FOLD)
    signs = (-1.0) ** np.arange(FOLDS)
    folded = (taper * signs[None, :, None]).transpose(1, 0, 2)
    return folded.astype(np.float32)


def transform_weights():
    odd = 2 * np.array(members(SPECTRA_FIRST)) + 1
    phase = (odd[:, None] * np.arange(FOLD)[None, :]) % (2 * FOLD)
    angle = phase.astype(np.float64) * (2.0 * np.pi / (2 * FOLD))
    scale = 1.0 / math.sqrt(NFFT)
    table = np.concatenate([np.cos(angle), -np.sin(angle)], axis=0) * scale
    high, low = split_bf16(table)
    return np.concatenate([high, low], axis=1)


GROUP = 8
GROUPS = SPECTRA // GROUP
TILES = 2 * OWNED


def channelize_kernel(
    volts_hbm, window_hbm, table_hbm, magnitude_hbm, phase_hbm, out_ref, model_ref,
    volts_ref, window_ref, table_ref, folded_ref, rows_ref, sems,
):
    def frames_copy(first, count, slot):
        span = pl.ds(first * NFFT, count * NFFT)
        return pltpu.make_async_copy(
            volts_hbm.at[:, span], volts_ref.at[:, span], sems.at[slot]
        )

    lead = TAPS - 1
    copies = [
        pltpu.make_async_copy(window_hbm, window_ref, sems.at[GROUPS]),
        frames_copy(0, lead, GROUPS + 1),
    ]
    model_copies = [
        pltpu.make_async_copy(
            magnitude_hbm, model_ref.at[pl.ds(0, TILES), :], sems.at[GROUPS + 2]
        ),
        pltpu.make_async_copy(
            phase_hbm, model_ref.at[pl.ds(TILES, TILES), :], sems.at[GROUPS + 3]
        ),
    ]
    table_copy = pltpu.make_async_copy(table_hbm, table_ref, sems.at[GROUPS + 4])
    for copy in copies:
        copy.start()
    for group in range(GROUPS):
        frames_copy(group * GROUP + lead, GROUP, group).start()
    for copy in [table_copy] + model_copies:
        copy.start()
    for copy in copies:
        copy.wait()

    def group_step(group):
        first = group * GROUP
        frames_copy(first + lead, GROUP, group).wait()
        for part in range(FOLD // 128):
            lanes = slice(part * 128, part * 128 + 128)
            sums = [jnp.zeros((OWNED, 128), F32)] * GROUP
            for fold in range(FOLDS):
                taps = [
                    jnp.broadcast_to(window_ref[fold, tap : tap + 1, lanes], (OWNED, 128))
                    for tap in range(TAPS)
                ]
                for frame in range(GROUP + TAPS - 1):
                    offset = (first + frame) * NFFT + fold * FOLD + part * 128
                    piece = volts_ref[:, pl.ds(offset, 128)]
                    piece = piece.astype(F32)
                    for tap in range(TAPS):
                        s = frame - tap
                        if 0 <= s < GROUP:
                            sums[s] = sums[s] + piece * taps[tap]
            for s in range(GROUP):
                row = (first + s) * OWNED
                folded_ref[part, pl.ds(row, OWNED), :] = sums[s]

    for group in range(GROUPS):
        group_step(group)
    pieces = []
    for part in range(FOLD // 128):
        pieces.append(
            jnp.concatenate(
                [folded_ref[part, pl.ds(j, SPECTRA, OWNED), :] for j in range(OWNED)],
                axis=0,
            )
        )
    folded = jnp.concatenate(pieces, axis=1)
    high = folded.astype(BF16)
    low = (folded - high.astype(F32)).astype(BF16)
    table_copy.wait()
    across = (((1,), (1,)), ((), ()))
    spectra = (
        lax.dot_general(table_ref[:, 0:FOLD], high, across, preferred_element_type=F32)
        + lax.dot_general(table_ref[:, 0:FOLD], low, across, preferred_element_type=F32)
        + lax.dot_general(
            table_ref[:, FOLD : 2 * FOLD], high, across, preferred_element_type=F32
        )
    )
    for part in range(2):
        for side in range(2):
            rows_ref[pl.ds(part * 2 + side, CHANNELS, 4), :] = spectra[
                part * CHANNELS : (part + 1) * CHANNELS, side * 128 : side * 128 + 128
            ]
    out_ref[...] = rows_ref[...].astype(BF16)
    for copy in model_copies:
        copy.wait()


def channelize(volts, magnitude, phase):
    operands = (
        volts,
        jnp.asarray(fold_weights()),
        jnp.asarray(transform_weights()),
        magnitude.reshape(TILES, 128),
        phase.reshape(TILES, 128),
    )
    return pl.pallas_call(
        channelize_kernel,
        out_shape=[
            pltpu.VMEM((CHANNELS * 4, 128), BF16),
            pltpu.VMEM((2 * TILES, 128), F32),
        ],
        in_specs=[pl.BlockSpec(memory_space=pltpu.HBM)] * 5,
        scratch_shapes=[
            pltpu.VMEM(volts.shape, BF16),
            pltpu.VMEM((FOLDS, TAPS, FOLD), F32),
            pltpu.VMEM((2 * CHANNELS, 2 * FOLD), BF16),
            pltpu.VMEM((2, SPECTRA * OWNED, 128), F32),
            pltpu.VMEM((CHANNELS * 4, 128), F32),
            pltpu.SemaphoreType.DMA((GROUPS + 5,)),
        ],
        compiler_params=pltpu.CompilerParams(vmem_limit_bytes=8 * 2**20),
        name="channelize",
    )(*[pltpu.with_memory_space_constraint(x, pltpu.HBM) for x in operands])


def turn_spectra(source, wide_ref, real_ref, imag_ref):
    wide_ref[...] = source[...].astype(F32)
    unswap(wide_ref, 4, SPECTRA_FIRST)
    for part, target in ((0, real_ref), (1, imag_ref)):
        for group in range(2):
            block = wide_ref[pl.ds(part * 2 + group, 128, 4), :].T
            for j in range(4):
                target[group * 4 + j] = block[j * 32 : j * 32 + 32, :]


def build_lines(wide_ref, line_ref):
    lane = lax.broadcasted_iota(jnp.int32, (128, 128), 1)
    for group in range(2):
        real = wide_ref[pl.ds(group, 128, 4), :]
        imag = wide_ref[pl.ds(2 + group, 128, 4), :]
        for j in range(4):
            a = real if j == 0 else pltpu.roll(real, 128 - 32 * j, 1)
            b = imag if j == 1 else pltpu.roll(imag, (160 - 32 * j) % 128, 1)
            line_ref[pl.ds(group * 4 + j, 128, OWNED), :] = jnp.where(lane < 32, a, b)


def build_right(line_ref, right_ref):
    for block in range(HALF // 128):
        columns = slice(block * 128, block * 128 + 128)
        turned = line_ref[columns, :].T
        real, imag = turned[0:32].astype(BF16), turned[32:64].astype(BF16)
        right_ref[0, 0:32, columns] = real
        right_ref[0, 32:64, columns] = imag
        right_ref[1, 0:32, columns] = -imag
        right_ref[1, 32:64, columns] = real


def own_kernel(
    own_ref, raw_ref, real_ref, imag_ref, left_ref, right_ref, model_ref,
    wide_ref, line_ref,
):
    magnitude, phase = raw_ref[0:TILES, :], raw_ref[TILES : 2 * TILES, :]
    model_ref[0:TILES, :] = magnitude * jnp.cos(phase)
    model_ref[TILES : 2 * TILES, :] = magnitude * jnp.sin(phase)
    model_ref[2 * TILES : 3 * TILES, :] = 1.0 / (magnitude * magnitude)
    turn_spectra(own_ref, wide_ref, real_ref, imag_ref)
    build_lines(wide_ref, line_ref)
    left_ref[...] = (line_ref[:, 0:64] * (1.0 / SPECTRA)).astype(BF16)
    build_right(line_ref, right_ref)


def own_turn(own, raw):
    return pl.pallas_call(
        own_kernel,
        out_shape=[
            pltpu.VMEM((OWNED, SPECTRA, 128), F32),
            pltpu.VMEM((OWNED, SPECTRA, 128), F32),
            pltpu.VMEM((HALF, 2 * SPECTRA), BF16),
            pltpu.VMEM((2, 2 * SPECTRA, HALF), BF16),
            pltpu.VMEM((3 * TILES, 128), F32),
        ],
        scratch_shapes=[pltpu.VMEM((512, 128), F32), pltpu.VMEM((HALF, 128), F32)],
        compiler_params=pltpu.CompilerParams(vmem_limit_bytes=8 * 2**20),
        cost_estimate=pl.CostEstimate(
            flops=2**22, bytes_accessed=2**20, transcendentals=0
        ),
        name="own_turn",
    )(own, raw)


def solve_kernel(
    ownr_ref, owni_ref, other_ref, model_ref, out_ref,
    wide_ref, otherr_ref, otheri_ref, probe_ref, part_ref,
):
    turn_spectra(other_ref, wide_ref, otherr_ref, otheri_ref)
    tiles = 2 * OWNED

    def spectra_of(tile):
        if tile < OWNED:
            return ownr_ref[tile], owni_ref[tile]
        return otherr_ref[tile - OWNED], otheri_ref[tile - OWNED]

    def gathered(which):
        total = part_ref[which, pl.ds(0, tiles, 8), :]
        for row in range(1, 8):
            total = total + part_ref[which, pl.ds(row, tiles, 8), :]
        return total

    def eight(values):
        return (values[0:8] + values[8:16]) + (values[16:24] + values[24:32])

    for tile in range(tiles):
        real, imag = spectra_of(tile)
        part_ref[0, tile * 8 : tile * 8 + 8, :] = eight(real * real + imag * imag)
    diagonal = gathered(0) * (1.0 / SPECTRA)
    half = lax.axis_index("bl")

    def model(which):
        rows = [
            pl.ds(pl.multiple_of(which * tiles + side * OWNED, OWNED), OWNED)
            for side in (half, 1 - half)
        ]
        return jnp.concatenate([model_ref[r, :] for r in rows], axis=0)

    mreal, mimag, inverse = model(0), model(1), model(2)

    def single_step(greal, gimag):
        yreal = greal * mreal - gimag * mimag
        yimag = greal * mimag + gimag * mreal
        energy = jnp.sum(yreal * yreal + yimag * yimag, keepdims=True) + EPSILON
        factor = inverse / energy
        probe_ref[0] = yreal
        probe_ref[1] = yimag
        areal = jnp.zeros((SPECTRA, 128), F32)
        aimag = jnp.zeros((SPECTRA, 128), F32)
        for tile in range(tiles):
            real, imag = spectra_of(tile)
            pr = jnp.broadcast_to(probe_ref[0, tile : tile + 1, :], (SPECTRA, 128))
            pi = jnp.broadcast_to(probe_ref[1, tile : tile + 1, :], (SPECTRA, 128))
            areal = areal + (real * pr + imag * pi)
            aimag = aimag + (real * pi - imag * pr)
        sreal = jnp.broadcast_to(jnp.sum(areal, axis=1, keepdims=True), (SPECTRA, 128))
        simag = jnp.broadcast_to(jnp.sum(aimag, axis=1, keepdims=True), (SPECTRA, 128))
        for tile in range(tiles):
            real, imag = spectra_of(tile)
            rows = slice(tile * 8, tile * 8 + 8)
            part_ref[0, rows, :] = eight(real * sreal - imag * simag)
            part_ref[1, rows, :] = eight(real * simag + imag * sreal)
        wreal = gathered(0) * (1.0 / SPECTRA) - diagonal * yreal
        wimag = gathered(1) * (1.0 / SPECTRA) - diagonal * yimag
        return (
            (wreal * mreal + wimag * mimag) * factor,
            (wimag * mreal - wreal * mimag) * factor,
        )

    greal = jnp.ones((tiles, 128), F32)
    gimag = jnp.zeros((tiles, 128), F32)

    for _ in range(ITERS // 2):
        first = single_step(greal, gimag)
        fresh = single_step(*first)
        greal, gimag = [(a + b) * 0.5 for a, b in zip(fresh, first)]
    wide_ref[0:128, :] = jnp.zeros((128, 128), F32)
    wide_ref[0:8, :] = greal[0:OWNED, :]
    wide_ref[8:16, :] = gimag[0:OWNED, :]
    out_ref[...] = wide_ref[0:128, :].T
    unswap(out_ref, 1, GAINS_FIRST)


def solve(ownr, owni, other, model):
    tiles = 2 * OWNED
    return pl.pallas_call(
        solve_kernel,
        out_shape=pltpu.VMEM((128, 128), F32),
        scratch_shapes=[
            pltpu.VMEM((512, 128), F32),
            pltpu.VMEM((OWNED, SPECTRA, 128), F32),
            pltpu.VMEM((OWNED, SPECTRA, 128), F32),
            pltpu.VMEM((2, tiles, 128), F32),
            pltpu.VMEM((2, tiles * 8, 128), F32),
        ],
        compiler_params=pltpu.CompilerParams(vmem_limit_bytes=8 * 2**20),
        name="solve",
    )(ownr, owni, other, model)


WIDE = 1024
SLOTS = 4


def power_kernel(
    left_ref, mine_ref, other_ref, out_hbm, wide_ref, line_ref, right_ref, slots_ref, sems
):
    half = lax.axis_index("bl")
    pieces = HALF // WIDE

    def out_copy(count, part, start):
        slot = lax.rem(count, SLOTS)
        columns = pl.ds(pl.multiple_of(start, WIDE), WIDE)
        return pltpu.make_async_copy(
            slots_ref.at[slot], out_hbm.at[part, :, columns], sems.at[slot]
        )

    def products(right, side, done):
        def step(index, carry):
            part, piece = index // pieces, lax.rem(index, pieces)
            count = done + index
            first = pl.multiple_of(piece * WIDE, WIDE)
            copy = out_copy(count, part, side * HALF + first)

            @pl.when(count >= SLOTS)
            def _():
                copy.wait()

            slots_ref[lax.rem(count, SLOTS)] = jnp.dot(
                left_ref[...], right[part, :, pl.ds(first, WIDE)],
                preferred_element_type=F32,
            ).astype(BF16)
            copy.start()
            return carry

        lax.fori_loop(0, 2 * pieces, step, 0)

    products(mine_ref, half, 0)
    wide_ref[...] = other_ref[...].astype(F32)
    unswap(wide_ref, 4, SPECTRA_FIRST)
    build_lines(wide_ref, line_ref)
    build_right(line_ref, right_ref)
    products(right_ref, 1 - half, 2 * pieces)
    for slot in range(SLOTS):
        out_copy(slot, 0, 0).wait()


def power(left, mine, other):
    return pl.pallas_call(
        power_kernel,
        in_specs=[pl.BlockSpec(memory_space=pltpu.VMEM)] * 3,
        out_specs=pl.BlockSpec(memory_space=pltpu.HBM),
        out_shape=jax.ShapeDtypeStruct((2, HALF, 2 * HALF), BF16),
        scratch_shapes=[
            pltpu.VMEM((512, 128), F32),
            pltpu.VMEM((HALF, 128), F32),
            pltpu.VMEM((2, 2 * SPECTRA, HALF), BF16),
            pltpu.VMEM((SLOTS, HALF, WIDE), BF16),
            pltpu.SemaphoreType.DMA((SLOTS,)),
        ],
        compiler_params=pltpu.CompilerParams(vmem_limit_bytes=24 * 2**20),
        cost_estimate=pl.CostEstimate(
            flops=2 * 2 * 1024 * 2048 * 64, bytes_accessed=9 * 2**20, transcendentals=0
        ),
        name="power",
    )(left, mine, other)


def turn_kernel(gains_ref, out_ref, rows_ref):
    rows_ref[...] = gains_ref[...]
    unswap(rows_ref, 1, GAINS_FIRST)
    turned = rows_ref[...].T
    out_ref[0, 0] = turned[0:8, :]
    out_ref[1, 0] = turned[8:16, :]


def on_device(voltages, model_magnitude, model_phase):
    spectra, raw = channelize(voltages[0], model_magnitude, model_phase)
    own = exchange(spectra.reshape(CHANNELS, 4, 128), SPECTRA_FIRST)
    own = own.reshape(512, 128)
    other = lax.ppermute(own, "bl", [(0, 1), (1, 0)])
    ownr, owni, left, mine, model = own_turn(own, raw)
    model = model.reshape(6, 128, OWNED).transpose(0, 2, 1).reshape(3 * TILES, 128)
    gains = solve(ownr, owni, other, model)
    moved = exchange(gains.reshape(128, 1, 128), GAINS_FIRST)
    visible = power(left, mine, other)
    gain_output = pl.pallas_call(
        turn_kernel,
        out_shape=jax.ShapeDtypeStruct((2, 1, OWNED, CHANNELS), F32),
        scratch_shapes=[pltpu.VMEM((128, 128), F32)],
        compiler_params=pltpu.CompilerParams(vmem_limit_bytes=2 * 2**20),
        name="turn",
    )(moved.reshape(128, 128))
    return visible[None], gain_output


def solution(mesh):
    in_specs = (P("bl", "gx", None), P("gx", None), P("gx", None))
    out_specs = (P("gx", None, "bl", None), P(None, "bl", "gx", None))
    return jax.shard_map(
        on_device, mesh=mesh, in_specs=in_specs, out_specs=out_specs, check_vma=False
    )
```

```python
import functools
import math

import jax
import jax.numpy as jnp
import numpy as np
from jax import lax
from jax.experimental import pallas as pl
from jax.experimental.pallas import tpu as pltpu
from jax.sharding import PartitionSpec as P

NFFT = 2048
TAPS = 4
SPECTRA = 32
ITERS = 4
CHANNELS = 128
OWNED = 8
HALF = 1024
EPSILON = 1e-06
F32 = jnp.float32
BF16 = jnp.bfloat16
FOLD = 256
FOLDS = NFFT // FOLD


SPECTRA_FIRST = 90
GAINS_FIRST = 22


def members(first):
    order = list(range(CHANNELS))
    order[0], order[first] = order[first], order[0]
    return order


def exchange(values, first):
    return lax.all_to_all(values, "gx", 0, 0, axis_index_groups=[members(first)])


def unswap(ref, rows, first):
    here, there = slice(0, rows), slice(first * rows, (first + 1) * rows)
    one, two = ref[here, :], ref[there, :]
    ref[here, :] = two
    ref[there, :] = one


def split_bf16(values):
    high = values.astype(np.float32).astype(jnp.bfloat16)
    low = (values - high.astype(np.float64)).astype(np.float32).astype(jnp.bfloat16)
    return high, low


def fold_weights():
    position = np.arange(TAPS * NFFT, dtype=np.float64) + 0.5
    hann = 0.5 - 0.5 * np.cos(2.0 * np.pi * position / (TAPS * NFFT))
    taper = np.sinc(position / NFFT - TAPS / 2.0) * hann
    taper = taper.reshape(TAPS, FOLDS, FOLD)
    signs = (-1.0) ** np.arange(FOLDS)
    folded = (taper * signs[None, :, None]).transpose(1, 0, 2)
    return folded.astype(np.float32)


def transform_weights():
    odd = 2 * np.array(members(SPECTRA_FIRST)) + 1
    phase = (odd[:, None] * np.arange(FOLD)[None, :]) % (2 * FOLD)
    angle = phase.astype(np.float64) * (2.0 * np.pi / (2 * FOLD))
    scale = 1.0 / math.sqrt(NFFT)
    table = np.concatenate([np.cos(angle), -np.sin(angle)], axis=0) * scale
    high, low = split_bf16(table)
    return np.concatenate([high, low], axis=1)


GROUP = 8
GROUPS = SPECTRA // GROUP
TILES = 2 * OWNED


def channelize_kernel(
    volts_hbm, window_hbm, table_hbm, magnitude_hbm, phase_hbm, out_ref, model_ref,
    volts_ref, window_ref, table_ref, folded_ref, rows_ref, sems,
):
    def frames_copy(first, count, slot):
        span = pl.ds(first * NFFT, count * NFFT)
        return pltpu.make_async_copy(
            volts_hbm.at[:, span], volts_ref.at[:, span], sems.at[slot]
        )

    lead = TAPS - 1
    copies = [
        pltpu.make_async_copy(window_hbm, window_ref, sems.at[GROUPS]),
        frames_copy(0, lead, GROUPS + 1),
    ]
    model_copies = [
        pltpu.make_async_copy(
            magnitude_hbm, model_ref.at[pl.ds(0, TILES), :], sems.at[GROUPS + 2]
        ),
        pltpu.make_async_copy(
            phase_hbm, model_ref.at[pl.ds(TILES, TILES), :], sems.at[GROUPS + 3]
        ),
    ]
    table_copy = pltpu.make_async_copy(table_hbm, table_ref, sems.at[GROUPS + 4])
    for copy in copies:
        copy.start()
    for group in range(GROUPS):
        frames_copy(group * GROUP + lead, GROUP, group).start()
    for copy in [table_copy] + model_copies:
        copy.start()
    for copy in copies:
        copy.wait()

    def group_step(group):
        first = group * GROUP
        frames_copy(first + lead, GROUP, group).wait()
        for part in range(FOLD // 128):
            lanes = slice(part * 128, part * 128 + 128)
            sums = [jnp.zeros((OWNED, 128), F32)] * GROUP
            for fold in range(FOLDS):
                taps = [
                    jnp.broadcast_to(window_ref[fold, tap : tap + 1, lanes], (OWNED, 128))
                    for tap in range(TAPS)
                ]
                for frame in range(GROUP + TAPS - 1):
                    offset = (first + frame) * NFFT + fold * FOLD + part * 128
                    piece = volts_ref[:, pl.ds(offset, 128)]
                    piece = piece.astype(F32)
                    for tap in range(TAPS):
                        s = frame - tap
                        if 0 <= s < GROUP:
                            sums[s] = sums[s] + piece * taps[tap]
            for s in range(GROUP):
                row = (first + s) * OWNED
                folded_ref[part, pl.ds(row, OWNED), :] = sums[s]

    for group in range(GROUPS):
        group_step(group)
    pieces = []
    for part in range(FOLD // 128):
        pieces.append(
            jnp.concatenate(
                [folded_ref[part, pl.ds(j, SPECTRA, OWNED), :] for j in range(OWNED)],
                axis=0,
            )
        )
    folded = jnp.concatenate(pieces, axis=1)
    high = folded.astype(BF16)
    low = (folded - high.astype(F32)).astype(BF16)
    table_copy.wait()
    across = (((1,), (1,)), ((), ()))
    spectra = (
        lax.dot_general(table_ref[:, 0:FOLD], high, across, preferred_element_type=F32)
        + lax.dot_general(table_ref[:, 0:FOLD], low, across, preferred_element_type=F32)
        + lax.dot_general(
            table_ref[:, FOLD : 2 * FOLD], high, across, preferred_element_type=F32
        )
    )
    for part in range(2):
        for side in range(2):
            rows_ref[pl.ds(part * 2 + side, CHANNELS, 4), :] = spectra[
                part * CHANNELS : (part + 1) * CHANNELS, side * 128 : side * 128 + 128
            ]
    out_ref[...] = rows_ref[...].astype(BF16)
    for copy in model_copies:
        copy.wait()


def channelize(volts, magnitude, phase):
    operands = (
        volts,
        jnp.asarray(fold_weights()),
        jnp.asarray(transform_weights()),
        magnitude.reshape(TILES, 128),
        phase.reshape(TILES, 128),
    )
    return pl.pallas_call(
        channelize_kernel,
        out_shape=[
            pltpu.VMEM((CHANNELS * 4, 128), BF16),
            pltpu.VMEM((2 * TILES, 128), F32),
        ],
        in_specs=[pl.BlockSpec(memory_space=pltpu.HBM)] * 5,
        scratch_shapes=[
            pltpu.VMEM(volts.shape, BF16),
            pltpu.VMEM((FOLDS, TAPS, FOLD), F32),
            pltpu.VMEM((2 * CHANNELS, 2 * FOLD), BF16),
            pltpu.VMEM((2, SPECTRA * OWNED, 128), F32),
            pltpu.VMEM((CHANNELS * 4, 128), F32),
            pltpu.SemaphoreType.DMA((GROUPS + 5,)),
        ],
        compiler_params=pltpu.CompilerParams(vmem_limit_bytes=8 * 2**20),
        name="channelize",
    )(*[pltpu.with_memory_space_constraint(x, pltpu.HBM) for x in operands])


def turn_spectra(source, wide_ref, real_ref, imag_ref):
    wide_ref[...] = source[...].astype(F32)
    unswap(wide_ref, 4, SPECTRA_FIRST)
    for part, target in ((0, real_ref), (1, imag_ref)):
        for group in range(2):
            block = wide_ref[pl.ds(part * 2 + group, 128, 4), :].T
            for j in range(4):
                target[group * 4 + j] = block[j * 32 : j * 32 + 32, :]


def build_lines(wide_ref, line_ref):
    lane = lax.broadcasted_iota(jnp.int32, (128, 128), 1)
    for group in range(2):
        real = wide_ref[pl.ds(group, 128, 4), :]
        imag = wide_ref[pl.ds(2 + group, 128, 4), :]
        for j in range(4):
            a = real if j == 0 else pltpu.roll(real, 128 - 32 * j, 1)
            b = imag if j == 1 else pltpu.roll(imag, (160 - 32 * j) % 128, 1)
            line_ref[pl.ds(group * 4 + j, 128, OWNED), :] = jnp.where(lane < 32, a, b)


def build_right(line_ref, right_ref):
    for block in range(HALF // 128):
        columns = slice(block * 128, block * 128 + 128)
        turned = line_ref[columns, :].T
        real, imag = turned[0:32].astype(BF16), turned[32:64].astype(BF16)
        right_ref[0, 0:32, columns] = real
        right_ref[0, 32:64, columns] = imag
        right_ref[1, 0:32, columns] = -imag
        right_ref[1, 32:64, columns] = real


def own_kernel(
    own_ref, raw_ref, real_ref, imag_ref, left_ref, right_ref, model_ref,
    wide_ref, line_ref,
):
    magnitude, phase = raw_ref[0:TILES, :], raw_ref[TILES : 2 * TILES, :]
    model_ref[0:TILES, :] = magnitude * jnp.cos(phase)
    model_ref[TILES : 2 * TILES, :] = magnitude * jnp.sin(phase)
    model_ref[2 * TILES : 3 * TILES, :] = 1.0 / (magnitude * magnitude)
    turn_spectra(own_ref, wide_ref, real_ref, imag_ref)
    build_lines(wide_ref, line_ref)
    left_ref[...] = (line_ref[:, 0:64] * (1.0 / SPECTRA)).astype(BF16)
    build_right(line_ref, right_ref)


def own_turn(own, raw):
    return pl.pallas_call(
        own_kernel,
        out_shape=[
            pltpu.VMEM((OWNED, SPECTRA, 128), F32),
            pltpu.VMEM((OWNED, SPECTRA, 128), F32),
            pltpu.VMEM((HALF, 2 * SPECTRA), BF16),
            pltpu.VMEM((2, 2 * SPECTRA, HALF), BF16),
            pltpu.VMEM((3 * TILES, 128), F32),
        ],
        scratch_shapes=[pltpu.VMEM((512, 128), F32), pltpu.VMEM((HALF, 128), F32)],
        compiler_params=pltpu.CompilerParams(vmem_limit_bytes=8 * 2**20),
        cost_estimate=pl.CostEstimate(
            flops=2**22, bytes_accessed=2**20, transcendentals=0
        ),
        name="own_turn",
    )(own, raw)


def solve_kernel(
    ownr_ref, owni_ref, other_ref, model_ref, out_ref,
    wide_ref, otherr_ref, otheri_ref, probe_ref, part_ref,
):
    turn_spectra(other_ref, wide_ref, otherr_ref, otheri_ref)
    tiles = 2 * OWNED

    def spectra_of(tile):
        if tile < OWNED:
            return ownr_ref[tile], owni_ref[tile]
        return otherr_ref[tile - OWNED], otheri_ref[tile - OWNED]

    def gathered(which):
        total = part_ref[which, pl.ds(0, tiles, 8), :]
        for row in range(1, 8):
            total = total + part_ref[which, pl.ds(row, tiles, 8), :]
        return total

    def eight(values):
        return (values[0:8] + values[8:16]) + (values[16:24] + values[24:32])

    for tile in range(tiles):
        real, imag = spectra_of(tile)
        part_ref[0, tile * 8 : tile * 8 + 8, :] = eight(real * real + imag * imag)
    diagonal = gathered(0) * (1.0 / SPECTRA)
    half = lax.axis_index("bl")

    def model(which):
        rows = [
            pl.ds(pl.multiple_of(which * tiles + side * OWNED, OWNED), OWNED)
            for side in (half, 1 - half)
        ]
        return jnp.concatenate([model_ref[r, :] for r in rows], axis=0)

    mreal, mimag, inverse = model(0), model(1), model(2)

    def single_step(greal, gimag):
        yreal = greal * mreal - gimag * mimag
        yimag = greal * mimag + gimag * mreal
        energy = jnp.sum(yreal * yreal + yimag * yimag, keepdims=True) + EPSILON
        factor = inverse / energy
        probe_ref[0] = yreal
        probe_ref[1] = yimag
        areal = jnp.zeros((SPECTRA, 128), F32)
        aimag = jnp.zeros((SPECTRA, 128), F32)
        for tile in range(tiles):
            real, imag = spectra_of(tile)
            pr = jnp.broadcast_to(probe_ref[0, tile : tile + 1, :], (SPECTRA, 128))
            pi = jnp.broadcast_to(probe_ref[1, tile : tile + 1, :], (SPECTRA, 128))
            areal = areal + (real * pr + imag * pi)
            aimag = aimag + (real * pi - imag * pr)
        sreal = jnp.broadcast_to(jnp.sum(areal, axis=1, keepdims=True), (SPECTRA, 128))
        simag = jnp.broadcast_to(jnp.sum(aimag, axis=1, keepdims=True), (SPECTRA, 128))
        for tile in range(tiles):
            real, imag = spectra_of(tile)
            rows = slice(tile * 8, tile * 8 + 8)
            part_ref[0, rows, :] = eight(real * sreal - imag * simag)
            part_ref[1, rows, :] = eight(real * simag + imag * sreal)
        wreal = gathered(0) * (1.0 / SPECTRA) - diagonal * yreal
        wimag = gathered(1) * (1.0 / SPECTRA) - diagonal * yimag
        return (
            (wreal * mreal + wimag * mimag) * factor,
            (wimag * mreal - wreal * mimag) * factor,
        )

    greal = jnp.ones((tiles, 128), F32)
    gimag = jnp.zeros((tiles, 128), F32)

    for _ in range(ITERS // 2):
        first = single_step(greal, gimag)
        fresh = single_step(*first)
        greal, gimag = [(a + b) * 0.5 for a, b in zip(fresh, first)]
    wide_ref[0:128, :] = jnp.zeros((128, 128), F32)
    wide_ref[0:8, :] = greal[0:OWNED, :]
    wide_ref[8:16, :] = gimag[0:OWNED, :]
    out_ref[...] = wide_ref[0:128, :].T
    unswap(out_ref, 1, GAINS_FIRST)


def solve(ownr, owni, other, model):
    tiles = 2 * OWNED
    return pl.pallas_call(
        solve_kernel,
        out_shape=pltpu.VMEM((128, 128), F32),
        scratch_shapes=[
            pltpu.VMEM((512, 128), F32),
            pltpu.VMEM((OWNED, SPECTRA, 128), F32),
            pltpu.VMEM((OWNED, SPECTRA, 128), F32),
            pltpu.VMEM((2, tiles, 128), F32),
            pltpu.VMEM((2, tiles * 8, 128), F32),
        ],
        compiler_params=pltpu.CompilerParams(vmem_limit_bytes=8 * 2**20),
        name="solve",
    )(ownr, owni, other, model)


WIDE = 1024
SLOTS = 4


def power_kernel(
    left_ref, mine_ref, other_ref, out_hbm, wide_ref, line_ref, right_ref, slots_ref, sems
):
    half = lax.axis_index("bl")
    pieces = HALF // WIDE

    def out_copy(count, part, start):
        slot = lax.rem(count, SLOTS)
        columns = pl.ds(pl.multiple_of(start, WIDE), WIDE)
        return pltpu.make_async_copy(
            slots_ref.at[slot], out_hbm.at[part, :, columns], sems.at[slot]
        )

    def products(right, side, done):
        def step(index, carry):
            part, piece = index // pieces, lax.rem(index, pieces)
            count = done + index
            first = pl.multiple_of(piece * WIDE, WIDE)
            copy = out_copy(count, part, side * HALF + first)

            @pl.when(count >= SLOTS)
            def _():
                copy.wait()

            slots_ref[lax.rem(count, SLOTS)] = jnp.dot(
                left_ref[...], right[part, :, pl.ds(first, WIDE)],
                preferred_element_type=F32,
            ).astype(BF16)
            copy.start()
            return carry

        lax.fori_loop(0, 2 * pieces, step, 0)

    products(mine_ref, half, 0)
    wide_ref[...] = other_ref[...].astype(F32)
    unswap(wide_ref, 4, SPECTRA_FIRST)
    build_lines(wide_ref, line_ref)
    build_right(line_ref, right_ref)
    products(right_ref, 1 - half, 2 * pieces)
    for slot in range(SLOTS):
        out_copy(slot, 0, 0).wait()


def power(left, mine, other):
    return pl.pallas_call(
        power_kernel,
        in_specs=[pl.BlockSpec(memory_space=pltpu.VMEM)] * 3,
        out_specs=pl.BlockSpec(memory_space=pltpu.HBM),
        out_shape=jax.ShapeDtypeStruct((2, HALF, 2 * HALF), BF16),
        scratch_shapes=[
            pltpu.VMEM((512, 128), F32),
            pltpu.VMEM((HALF, 128), F32),
            pltpu.VMEM((2, 2 * SPECTRA, HALF), BF16),
            pltpu.VMEM((SLOTS, HALF, WIDE), BF16),
            pltpu.SemaphoreType.DMA((SLOTS,)),
        ],
        compiler_params=pltpu.CompilerParams(vmem_limit_bytes=24 * 2**20),
        cost_estimate=pl.CostEstimate(
            flops=2 * 2 * 1024 * 2048 * 64, bytes_accessed=9 * 2**20, transcendentals=0
        ),
        name="power",
    )(left, mine, other)


def turn_kernel(gains_ref, out_ref, rows_ref):
    rows_ref[...] = gains_ref[...]
    unswap(rows_ref, 1, GAINS_FIRST)
    turned = rows_ref[...].T
    out_ref[0, 0] = turned[0:8, :]
    out_ref[1, 0] = turned[8:16, :]


def on_device(voltages, model_magnitude, model_phase):
    spectra, raw = channelize(voltages[0], model_magnitude, model_phase)
    own = exchange(spectra.reshape(CHANNELS, 4, 128), SPECTRA_FIRST)
    own = own.reshape(512, 128)
    other = lax.ppermute(own, "bl", [(0, 1), (1, 0)])
    ownr, owni, left, mine, model = own_turn(own, raw)
    model = model.reshape(6, 128, OWNED).transpose(0, 2, 1).reshape(3 * TILES, 128)
    gains = solve(ownr, owni, other, model)
    moved = exchange(gains.reshape(128, 1, 128), GAINS_FIRST)
    visible = power(left, mine, other)
    gain_output = pl.pallas_call(
        turn_kernel,
        out_shape=jax.ShapeDtypeStruct((2, 1, OWNED, CHANNELS), F32),
        scratch_shapes=[pltpu.VMEM((128, 128), F32)],
        compiler_params=pltpu.CompilerParams(vmem_limit_bytes=2 * 2**20),
        name="turn",
    )(moved.reshape(128, 128))
    return visible[None], gain_output


def solution(mesh):
    in_specs = (P("bl", "gx", None), P("gx", None), P("gx", None))
    out_specs = (P("gx", None, "bl", None), P(None, "bl", "gx", None))
    return jax.shard_map(
        on_device, mesh=mesh, in_specs=in_specs, out_specs=out_specs, check_vma=False
    )
```
